256 devices in a mesh: comp: 8 (over z_lo, core), cells: 32 (over z_hi, y, x).
Axes of the slice: x: 4, y: 4, z: 8 (z_hi: 2, z_lo: 4; z = z_hi * 4 + z_lo), core: 2. Of those that a mesh axis runs over, the one named last changes fastest.
Arguments:
- atm_flux: bfloat16 [72, 65536], P('comp', 'cells'), may hold values from -6 to 6
- level_weight: float32 [72], P('comp'), may hold values from 0.02 to 0.2
- tile_weight: bfloat16 [2048, 128, 128], P('cells'), may hold values from -0.25 to 0.25
- tile_source: int32 [2048], P('cells'), may hold values from 0 to 15
- tile_target: int32 [2048], P('cells'), may hold values from 0 to 15
- ocean_start: float32 [65536], P('cells'), may hold values from -6 to 6
- conductance: float32 [6, 65536], P(None, 'cells'), may hold values from 0.02 to 0.15
- damping: float32 [65536], P('cells'), may hold values from 0.05 to 0.3
- neighbors: int32 [6, 65536], P(None, 'cells'), may hold values from 0 to 2559
- send_lists: int32 [2, 8192], P(None, 'cells'), may hold values from 0 to 2047
Outputs:
- ocean_end: float32 [65536], P('cells')
- atm_surface: float32 [65536], P('cells')
The draws below stay inside these ranges and needn't reach their ends.
All inputs are finite; a program needn't handle non-finite values.
Results may differ from the reference program's by a relative error of at most 0.0003.
Values sent between devices are 32-bit elements; how exact they have to be, the bound alone decides.
No kernel may reach another device: no remote copies, remote signals or barrier semaphores. Data moves between devices by JAX's collectives and lax.ppermute only.
A program may use at most 64 MiB of HBM per device.

```python
import math
import jax
import jax.numpy as jnp
from jax import lax

LEV = 72
BS = 128
AB = 16
OB = 16
K = 2
HALO = 256
SUBSTEPS = 10
ACOLS = 65536
OCELLS = 65536
TILES = 2048
SENDS = 8192
N_CELLS = 32


def touch_ends(array, rng, least, top_value):
    place = [jax.random.randint(jax.random.fold_in(rng, axis), (), 0, length) for axis, length in enumerate(array.shape)]
    main_axis = array.shape.index(max(array.shape))
    next_to = place[:main_axis] + [(place[main_axis] + 1) % array.shape[main_axis]] + place[main_axis + 1:]
    return array.at[tuple(place)].set(least).at[tuple(next_to)].set(top_value)


def block_scale(stream_key, dims, cuts, low, largest):
    def one(dim, parts):
        heights = jax.random.uniform(jax.random.fold_in(jax.random.fold_in(stream_key, 6), dim), (parts,), jnp.float32, low / len(cuts), largest / len(cuts))
        return jnp.repeat(jnp.exp(heights), dims[dim] // parts).reshape((-1,) + (1,) * (len(dims) - dim - 1))

    loudness = one(*cuts[0])
    for cut in cuts[1:]:
        loudness = loudness * one(*cut)
    return loudness


def noise(key, shape, spread, reach, pieces=(), kind=jnp.bfloat16):
    gain = block_scale(key, shape, pieces, -0.22, 0.18) if pieces else 1.0
    array = jax.random.normal(key, shape, jnp.float32) * spread * gain
    return jnp.minimum(jnp.maximum(array, -reach), reach).astype(kind)


def setup_inputs(seed: int = 0) -> dict:
    keys = jax.random.split(jax.random.key(seed), 11)
    atm_flux = noise(keys[0], (LEV, ACOLS), 1.0, 6.0, ((0, 8), (1, 32)))
    level_weight = jnp.clip(jnp.exp(math.log(0.2) - 2.3025851 * jax.random.uniform(keys[1], (LEV,), jnp.float32) ** block_scale(keys[1], (LEV,), ((0, 8),), -0.2, 0.2)), 0.02, 0.2)
    tile_weight = noise(keys[2], (TILES, BS, BS), (BS * N_CELLS * K // AB) ** -0.5, 0.25, ((0, 32),))
    tile_source = touch_ends(jax.random.randint(keys[3], (TILES,), 0, AB), jax.random.fold_in(keys[3], 1), 0, AB - 1).astype(jnp.int32)
    tile_target = touch_ends(jax.random.randint(keys[4], (TILES,), 0, OB), jax.random.fold_in(keys[4], 1), 0, OB - 1).astype(jnp.int32)
    ocean_start = noise(keys[5], (OCELLS,), 1.0, 6.0, ((0, 32),), jnp.float32)
    conductance = jnp.clip(jnp.exp(math.log(0.15) - 2.014903 * jax.random.uniform(keys[6], (6, OCELLS), jnp.float32) ** block_scale(keys[6], (6, OCELLS), ((1, 32),), -0.2, 0.2)), 0.02, 0.15)
    damping = jnp.clip(jnp.exp(math.log(0.3) - 1.7917595 * jax.random.uniform(keys[7], (OCELLS,), jnp.float32) ** block_scale(keys[7], (OCELLS,), ((0, 32),), -0.2, 0.2)), 0.05, 0.3)
    neighbors = touch_ends(jax.random.randint(keys[8], (6, OCELLS), 0, OB * BS + 2 * HALO), jax.random.fold_in(keys[8], 1), 0, (OB * BS + 2 * HALO) - 1).astype(jnp.int32)
    send_lists = touch_ends(jax.random.randint(keys[9], (2, SENDS), 0, OB * BS), jax.random.fold_in(keys[9], 1), 0, (OB * BS) - 1).astype(jnp.int32)
    return {"atm_flux": atm_flux, "level_weight": level_weight, "tile_weight": tile_weight, "tile_source": tile_source, "tile_target": tile_target, "ocean_start": ocean_start, "conductance": conductance, "damping": damping, "neighbors": neighbors, "send_lists": send_lists}


def reference(atm_flux, level_weight, tile_weight, tile_source, tile_target, ocean_start, conductance, damping, neighbors, send_lists):
    highest = lax.Precision.HIGHEST
    groups = N_CELLS
    ocean_local = OB * BS
    weighted = jnp.einsum('l,lx->x', level_weight, atm_flux.astype(jnp.float32), precision=highest)
    atm_blocks = weighted.reshape(groups, AB, BS)
    source_rows = tile_source.reshape(groups, groups * K)
    picked = jax.vmap(lambda blocks, rows: blocks[rows])(atm_blocks, source_rows)
    weights = tile_weight.astype(jnp.float32).reshape(groups, groups * K, BS, BS)
    terms = jnp.einsum('srb,srbc->src', picked, weights, precision=highest)
    terms = terms.reshape(groups, groups, K, BS).transpose(1, 0, 2, 3).reshape(groups, groups * K, BS)
    target_rows = tile_target.reshape(groups, groups * K)
    target_hot = (target_rows[:, :, None] == jnp.arange(OB, dtype=jnp.int32)[None, None, :]).astype(jnp.float32)
    forcing = jnp.einsum('pro,prc->poc', target_hot, terms, precision=highest).reshape(groups, ocean_local)
    surface = ocean_start.reshape(groups, ocean_local)
    conduct_all = conductance.reshape(6, groups, ocean_local).transpose(1, 0, 2)
    nearest = neighbors.reshape(6, groups, ocean_local).transpose(1, 0, 2)
    send_rows = send_lists.reshape(2, groups, HALO)
    relax = damping.reshape(groups, ocean_local)
    for counter in range(SUBSTEPS):
        to_lower = jax.vmap(lambda field, rows: field[rows])(surface, send_rows[0])
        to_higher = jax.vmap(lambda field, rows: field[rows])(surface, send_rows[1])
        from_lower = jnp.roll(to_higher, 1, axis=0)
        from_higher = jnp.roll(to_lower, -1, axis=0)
        extended = jnp.concatenate([surface, from_lower, from_higher], axis=1)
        nearby = jax.vmap(lambda field, rows: field[rows])(extended, nearest)
        flowing = jnp.sum(conduct_all * (nearby - surface[:, None, :]), axis=1)
        surface = surface + flowing - relax * surface + forcing
    values = jnp.einsum('pro,poc->prc', target_hot, surface.reshape(groups, OB, BS), precision=highest)
    values = values.reshape(groups, groups, K, BS).transpose(1, 0, 2, 3).reshape(groups, groups * K, BS)
    pulled = jnp.einsum('src,srbc->srb', values, weights, precision=highest)
    source_hot = (source_rows[:, :, None] == jnp.arange(AB, dtype=jnp.int32)[None, None, :]).astype(jnp.float32)
    atm_back = jnp.einsum('sra,srb->sab', source_hot, pulled, precision=highest)
    return surface.reshape(-1), atm_back.reshape(-1)
```

```python
import functools

import jax
import jax.numpy as jnp
from jax import lax
from jax.experimental import pallas as pl
from jax.experimental.pallas import tpu as pltpu
from jax.sharding import PartitionSpec as P

SUBSTEPS = 10
LANES = 128


def shifted(block, axis, distance):
    n = lax.axis_size(axis)
    return lax.ppermute(block, axis, [((i - distance) % n, i) for i in range(n)])


def lane_pick(rows, lane):
    dims = lax.GatherDimensionNumbers(
        offset_dims=(),
        collapsed_slice_dims=(1,),
        start_index_map=(1,),
        operand_batching_dims=(0,),
        start_indices_batching_dims=(0,),
    )
    return lax.gather(
        rows,
        lane[..., None],
        dims,
        slice_sizes=(1, 1),
        mode=lax.GatherScatterMode.PROMISE_IN_BOUNDS,
    )


def table_pick(table_ref, first, count, row, lane):
    size = row.shape[0]
    total = jnp.zeros(row.shape, jnp.float32)
    for r in range(count):
        line = table_ref[pl.ds(first + r, size, stride=0), :]
        total = jnp.where(row == r, lane_pick(line, lane), total)
    return total


def send_kernel(surface_ref, list_ref, out_ref):
    index = list_ref[...]
    out_ref[...] = table_pick(surface_ref, 0, 16, index >> 7, index & 127)


def step_kernel(surface_ref, low_ref, high_ref, neighbor_ref, conduct_ref, keep_ref, forcing_ref, list_ref, out_ref, send_ref, table_ref):
    table_ref[0:16] = surface_ref[...]
    table_ref[16:18] = low_ref[...]
    table_ref[18:20] = high_ref[...]
    for h in range(2):
        part = slice(8 * h, 8 * h + 8)
        total = keep_ref[part] * surface_ref[part] + forcing_ref[part]
        for m in range(6):
            index = neighbor_ref[m, part]
            near = table_pick(table_ref, 0, 20, index >> 7, index & 127)
            total = total + conduct_ref[m, part] * near
        out_ref[part] = total
    index = list_ref[...]
    send_ref[...] = table_pick(out_ref, 0, 16, index >> 7, index & 127)


def local(
    atm_flux,
    level_weight,
    tile_weight,
    tile_source,
    tile_target,
    ocean_start,
    conductance,
    damping,
    neighbors,
    send_lists,
):
    highest = lax.Precision.HIGHEST
    block = tile_weight.shape[1]
    f32 = jnp.float32
    weights = tile_weight.astype(f32)
    source_hot = (tile_source[:, None] == jnp.arange(16, dtype=jnp.int32)[None, :]).astype(f32)
    target_hot = (tile_target[:, None] == jnp.arange(16, dtype=jnp.int32)[None, :]).astype(f32)
    partial = jnp.sum(level_weight[:, None] * atm_flux.astype(f32), axis=0).reshape(16, block)
    shares = lax.all_to_all(
        jnp.broadcast_to(partial[None], (8, 16, block)), "comp", split_axis=0, concat_axis=0, tiled=True
    )
    flux = jnp.sum(shares, axis=0)
    picked = jnp.einsum("ra,ab->rb", source_hot, flux, precision=highest)
    terms = jnp.sum(picked[:, :, None] * weights, axis=1)
    arrived = lax.all_to_all(terms, "cells", split_axis=0, concat_axis=0, tiled=True)
    forcing = jnp.einsum("ro,rc->oc", target_hot, arrived, precision=highest)

    keep = (1.0 - jnp.sum(conductance, axis=0) - damping).reshape(16, block)
    conduct = conductance.reshape(6, 16, block)
    near = neighbors.reshape(6, 16, block)
    lists = send_lists.reshape(4, block)
    surface = ocean_start.reshape(16, block)
    outgoing = pl.pallas_call(send_kernel, out_shape=jax.ShapeDtypeStruct((4, block), f32))(surface, lists)
    step = pl.pallas_call(
        step_kernel,
        out_shape=(jax.ShapeDtypeStruct((16, block), f32), jax.ShapeDtypeStruct((4, block), f32)),
        scratch_shapes=[pltpu.VMEM((20, block), f32)],
    )
    for _ in range(SUBSTEPS):
        from_lower = shifted(outgoing[2:4], "cells", 1)
        from_higher = shifted(outgoing[0:2], "cells", -1)
        surface, outgoing = step(surface, from_lower, from_higher, near, conduct, keep, forcing, lists)
    ocean_end = surface.reshape(-1)
    values = jnp.einsum("ro,oc->rc", target_hot, surface, precision=highest)
    returned = lax.all_to_all(values, "cells", split_axis=0, concat_axis=0, tiled=True)
    pulled = jnp.sum(returned[:, None, :] * weights, axis=2)
    atm_back = jnp.einsum("ra,rb->ab", source_hot, pulled, precision=highest).reshape(-1)
    return (ocean_end, atm_back)


def solution(mesh):
    in_specs = (
        P("comp", "cells"),
        P("comp"),
        P("cells", None, None),
        P("cells"),
        P("cells"),
        P("cells"),
        P(None, "cells"),
        P("cells"),
        P(None, "cells"),
        P(None, "cells"),
    )
    out_specs = (P("cells"), P("cells"))
    return jax.shard_map(local, mesh=mesh, in_specs=in_specs, out_specs=out_specs, check_vma=False)
```

```python
import functools

import jax
import jax.numpy as jnp
from jax import lax
from jax.experimental import pallas as pl
from jax.experimental.pallas import tpu as pltpu
from jax.sharding import PartitionSpec as P

LANES = 128
OWNERS = 32
HALF = 16
BLOCKS = 16
REACH = 4
STEPS = 5
WINDOW = 2 * REACH + 1
PART = 232
CONDUCT, KEEP, START, LISTS, TARGET = 96, 192, 208, 224, 228
TABLE = 24
SENT = 24
BOTH = ("comp", "cells")
HIGHEST = lax.Precision.HIGHEST
F32 = jnp.float32


def device_of(owner, copy, core):
    z_low = copy if owner < HALF else (copy + 2) % 4
    return (2 * z_low + core) * OWNERS + owner


COPIES = [(copy, core) for copy in range(4) for core in range(2)]
GROUPS = [[device_of(owner, *copy) for owner in range(OWNERS)] for copy in COPIES]


def from_owner(block, offset):
    route = [
        (device_of((owner + offset) % OWNERS, *copy), device_of(owner, *copy))
        for copy in COPIES
        for owner in range(OWNERS)
    ]
    return lax.ppermute(block, BOTH, route)


def between_owners(blocks):
    return lax.all_to_all(
        blocks, BOTH, split_axis=0, concat_axis=0, tiled=True, axis_index_groups=GROUPS
    )


def lane_pick(rows, lane):
    dims = lax.GatherDimensionNumbers(
        offset_dims=(),
        collapsed_slice_dims=(1,),
        start_index_map=(1,),
        operand_batching_dims=(0,),
        start_indices_batching_dims=(0,),
    )
    return lax.gather(
        rows,
        lane[..., None],
        dims,
        slice_sizes=(1, 1),
        mode=lax.GatherScatterMode.PROMISE_IN_BOUNDS,
    )


def table_pick(table_ref, count, index):
    row, lane = index >> 7, index & 127
    total = None
    for r in range(count):
        line = table_ref[pl.ds(r, index.shape[0], stride=0), :]
        near = lane_pick(line, lane)
        total = near if total is None else jnp.where(row == r, near, total)
    return total


def terms_kernel(shares_ref, source_ref, weight_ref, out_ref, parts_ref, terms_ref):
    flux = jnp.sum(shares_ref[...], axis=0)
    tiles = lax.broadcasted_iota(jnp.int32, (64, BLOCKS), 1)
    hot = (source_ref[...] == tiles).astype(F32)
    picked = jnp.dot(hot, flux, precision=HIGHEST, preferred_element_type=F32)
    high = picked.astype(jnp.bfloat16).astype(F32)
    rest = picked - high
    middle = rest.astype(jnp.bfloat16).astype(F32)
    parts_ref[...] = jnp.zeros_like(parts_ref)
    parts_ref[:, 0, :] = high
    parts_ref[:, 1, :] = middle
    parts_ref[:, 2, :] = rest - middle
    for t in range(64):
        left = parts_ref[t].astype(jnp.bfloat16)
        three = jnp.dot(left, weight_ref[t], preferred_element_type=F32)
        term = jnp.sum(three, axis=0, keepdims=True)
        place = (t + 2 * REACH) % 64
        while place < 64 + SENT:
            terms_ref[place : place + 1] = term
            place += 64
    for p in range(OWNERS):
        out_ref[p] = terms_ref[2 * p : 2 * p + SENT]


def send(table_ref, slot, lists_ref):
    index = lists_ref[pl.ds(pl.multiple_of((slot - 1) * 8, 8), 8), :].astype(jnp.int32)
    values = table_pick(table_ref.at[slot], 16, index)
    table_ref[slot - 1, 18:20] = values[0:2]
    table_ref[slot + 1, 16:18] = values[2:4]


def run_steps(tables, part_ref, lists_ref, forcing_ref):
    def first(slot, carry):
        send(tables[0], slot, lists_ref)
        return carry

    lax.fori_loop(1, WINDOW + 3, first, 0)
    for step in range(STEPS):
        left = STEPS - 1 - step
        old, new = tables[step % 2], tables[(step + 1) % 2]

        def advance(slot, carry, old=old, new=new, left=left):
            base = pl.multiple_of((slot - 2) * PART, 8)
            force = pl.multiple_of((slot - 2) * 16, 8)
            for h in range(2):
                own = old[slot, 8 * h : 8 * h + 8]
                total = part_ref[pl.ds(base + KEEP + 8 * h, 8), :] * own + forcing_ref[pl.ds(force + 8 * h, 8), :]
                for m in range(6):
                    index = part_ref[pl.ds(base + 16 * m + 8 * h, 8), :].astype(jnp.int32)
                    near = table_pick(old.at[slot], 20, index)
                    total = total + part_ref[pl.ds(base + CONDUCT + 16 * m + 8 * h, 8), :] * near
                new[slot, 8 * h : 8 * h + 8] = total
            if left:
                send(new, slot, lists_ref)
            return carry

        lax.fori_loop(REACH + 2 - left, REACH + 3 + left, advance, 0)
    return tables[STEPS % 2][REACH + 2, 0:16]


def first_kernel(arrived_ref, key_ref, part_ref, lists_ref, start_ref, forcing_ref, out_ref, table0, table1):
    owners = lax.broadcasted_iota(jnp.int32, (16 * WINDOW, OWNERS * SENT), 0)
    hot = (owners == key_ref[...]).astype(F32)
    terms = arrived_ref[...].reshape(OWNERS * SENT, LANES)
    forcing_ref[...] = jnp.dot(hot, terms, precision=HIGHEST, preferred_element_type=F32)
    for slot in range(1, WINDOW + 3):
        table0[slot, 0:16] = start_ref[16 * (slot - 1) : 16 * slot]
    surface = run_steps((table0, table1), part_ref, lists_ref, forcing_ref)
    out_ref[...] = jnp.broadcast_to(surface[None], out_ref.shape)


def last_kernel(owner_ref, surfaces_ref, target_ref, part_ref, lists_ref, forcing_ref, out_ref, values_ref, table0, table1):
    for slot in range(1, WINDOW + 3):
        owner = (owner_ref[0] + (slot - REACH - 2 + OWNERS)) % OWNERS
        table0[slot, 0:16] = surfaces_ref[owner]
    surface = run_steps((table0, table1), part_ref, lists_ref, forcing_ref)
    out_ref[...] = surface
    blocks = lax.broadcasted_iota(jnp.int32, (64, BLOCKS), 1)
    hot = (target_ref[...] == blocks).astype(F32)
    values_ref[...] = jnp.dot(hot, surface, precision=HIGHEST, preferred_element_type=F32)


def shape(*dims):
    return jax.ShapeDtypeStruct(dims, F32)


def local(
    atm_flux,
    level_weight,
    tile_weight,
    tile_source,
    tile_target,
    ocean_start,
    conductance,
    damping,
    neighbors,
    send_lists,
):
    tables = [pltpu.VMEM((WINDOW + 4, TABLE, LANES), F32)] * 2

    keep = 1.0 - jnp.sum(conductance, axis=0) - damping
    target_row = jnp.pad(tile_target.astype(F32), (0, 64)).reshape(1, LANES)
    packed = jnp.concatenate(
        [
            neighbors.astype(F32).reshape(96, LANES),
            conductance.reshape(96, LANES),
            keep.reshape(16, LANES),
            ocean_start.reshape(16, LANES),
            send_lists.astype(F32).reshape(4, LANES),
            target_row,
            jnp.zeros((3, LANES), F32),
        ],
        axis=0,
    )
    three = jnp.concatenate([from_owner(packed, -1), packed, from_owner(packed, 1)], axis=0)
    outer = packed[START : START + 24]
    below, above = from_owner(outer, -STEPS), from_owner(outer, STEPS)
    parts = jnp.concatenate([from_owner(three, -3), three, from_owner(three, 3)], axis=0)
    by_owner = parts.reshape(WINDOW, PART, LANES)
    starts = jnp.concatenate([below[:16], by_owner[:, START:LISTS].reshape(-1, LANES), above[:16]], axis=0)
    lists = jnp.concatenate([below[16:24], by_owner[:, LISTS:PART].reshape(-1, LANES), above[16:24]], axis=0)
    targets = by_owner[:, TARGET, :64].astype(jnp.int32) + 16 * jnp.arange(WINDOW, dtype=jnp.int32)[:, None]
    key = jnp.pad(
        targets.reshape(WINDOW, OWNERS, 2).transpose(1, 0, 2).reshape(OWNERS, 2 * WINDOW),
        ((0, 0), (0, SENT - 2 * WINDOW)),
        constant_values=-1,
    ).reshape(1, OWNERS * SENT)

    partial = jnp.sum(level_weight[:, None] * atm_flux.astype(F32), axis=0).reshape(BLOCKS, LANES)
    shares = lax.all_to_all(
        jnp.broadcast_to(partial[None], (8, BLOCKS, LANES)), "comp", split_axis=0, concat_axis=0, tiled=True
    )
    terms = pl.pallas_call(
        terms_kernel,
        out_shape=shape(OWNERS, SENT, LANES),
        scratch_shapes=[pltpu.VMEM((64, 8, LANES), F32), pltpu.VMEM((64 + SENT, LANES), F32)],
    )(shares, tile_source[:, None], tile_weight)
    arrived = between_owners(terms)

    forcing, surface = pl.pallas_call(
        first_kernel,
        out_shape=(shape(16 * WINDOW, LANES), shape(OWNERS, 16, LANES)),
        scratch_shapes=tables,
    )(arrived, key, parts, lists, starts)
    surfaces = between_owners(surface)
    owner = lax.axis_index("cells").astype(jnp.int32).reshape(1)
    vmem = pl.BlockSpec(memory_space=pltpu.VMEM)
    ocean_end, values = pl.pallas_call(
        last_kernel,
        out_shape=(shape(16, LANES), shape(64, LANES)),
        in_specs=[pl.BlockSpec(memory_space=pltpu.SMEM)] + [vmem] * 5,
        scratch_shapes=tables,
    )(owner, surfaces, tile_target[:, None], parts, lists, forcing)

    returned = between_owners(values.reshape(OWNERS, 2, LANES)).reshape(64, LANES)
    pulled = jnp.sum(returned[:, None, :] * tile_weight.astype(F32), axis=2)
    source_hot = (tile_source[:, None] == jnp.arange(BLOCKS, dtype=jnp.int32)[None, :]).astype(F32)
    atm_back = jnp.einsum("ra,rb->ab", source_hot, pulled, precision=HIGHEST).reshape(-1)
    return (ocean_end.reshape(-1), atm_back)


def solution(mesh):
    in_specs = (
        P("comp", "cells"),
        P("comp"),
        P("cells", None, None),
        P("cells"),
        P("cells"),
        P("cells"),
        P(None, "cells"),
        P("cells"),
        P(None, "cells"),
        P(None, "cells"),
    )
    out_specs = (P("cells"), P("cells"))
    return jax.shard_map(local, mesh=mesh, in_specs=in_specs, out_specs=out_specs, check_vma=False)
```

```python
import jax
import jax.numpy as jnp
from jax import lax
from jax.experimental import pallas as pl
from jax.experimental.pallas import tpu as pltpu
from jax.sharding import PartitionSpec as P

LANES = 128
OWNERS = 32
HALF = 16
TILES = 64
REACH = 4
STEPS = 5
WINDOW = 2 * REACH + 1
CENTER = REACH + 2
SLOTS = WINDOW + 4
PART = 232
CONDUCT, KEEP, START, LISTS, TARGET = 96, 192, 208, 224, 228
SENT = 40
TERMS = 22
BOTH = ("comp", "cells")
HIGHEST = lax.Precision.HIGHEST
F32, I32 = jnp.float32, jnp.int32
VMEM = pl.BlockSpec(memory_space=pltpu.VMEM)
SMEM = pl.BlockSpec(memory_space=pltpu.SMEM)


def device_of(owner, copy, core):
    z_low = copy if owner < HALF else 3 - copy
    return (2 * z_low + core) * OWNERS + owner


COPIES = [(copy, core) for copy in range(4) for core in range(2)]
ALL = [[device_of(owner, *copy) for owner in range(OWNERS)] for copy in COPIES]


def eights(first):
    return [
        [device_of((8 * g + first + i) % OWNERS, *copy) for i in range(8)] for copy in COPIES for g in range(4)
    ]


def exchange(blocks, groups):
    return lax.all_to_all(blocks, BOTH, split_axis=0, concat_axis=0, tiled=True, axis_index_groups=groups)


def lane_pick(rows, lane):
    dims = lax.GatherDimensionNumbers(
        offset_dims=(),
        collapsed_slice_dims=(1,),
        start_index_map=(1,),
        operand_batching_dims=(0,),
        start_indices_batching_dims=(0,),
    )
    return lax.gather(
        rows,
        lane[..., None],
        dims,
        slice_sizes=(1, 1),
        mode=lax.GatherScatterMode.PROMISE_IN_BOUNDS,
    )


def coded(index):
    row, lane = index >> 7, index & 127
    halo = row >= 16
    pair = jnp.where(halo, 8 + ((row >> 1) & 1), row & 7)
    half = jnp.where(halo, row & 1, row >> 3)
    return pair * 256 + half * 128 + lane


def pair_of(upper, lower):
    return (upper << 16) | (lower & 0xFFFF)


def pick(table_ref, count, code):
    lane, pair = code & 127, code >> 8
    total = None
    for r in range(count):
        line = table_ref[pl.ds(r, 8, stride=0), :]
        near = lane_pick(line, lane)
        total = near if total is None else jnp.where(pair == r, near, total)
    return jnp.where((code & 128) == 0, total, total << 16) >> 16


def prepare_kernel(weight_ref, flux_ref, neighbor_ref, conduct_ref, damping_ref, start_ref, lists_ref, target_ref, shares_ref, packed_ref, row_ref):
    for j in range(16):
        lanes = slice(LANES * j, LANES * j + LANES)
        block = flux_ref[:, lanes].astype(F32)
        row_ref[j : j + 1] = sum(weight_ref[level] * block[level : level + 1] for level in range(block.shape[0]))
    shares_ref[...] = jnp.broadcast_to(row_ref[...][None], shares_ref.shape)
    own = packed_ref.at[0]
    for j in range(16):
        lanes = slice(LANES * j, LANES * j + LANES)
        own[pl.ds(j, 6, stride=16), :] = coded(neighbor_ref[:, lanes]).astype(F32)
        conduct = conduct_ref[:, lanes]
        own[pl.ds(CONDUCT + j, 6, stride=16), :] = conduct
        own[KEEP + j : KEEP + j + 1] = 1.0 - jnp.sum(conduct, axis=0, keepdims=True) - damping_ref[j : j + 1]
    own[START:LISTS] = start_ref[...]
    for j in range(2):
        lanes = slice(LANES * j, LANES * j + LANES)
        lists = coded(lists_ref[:, lanes]).astype(F32)
        own[LISTS + j : LISTS + j + 1] = lists[0:1]
        own[LISTS + 2 + j : LISTS + 3 + j] = lists[1:2]
    own[TARGET:PART] = jnp.zeros((PART - TARGET, LANES), F32)
    own[TARGET : TARGET + 1, 0:TILES] = target_ref[...].astype(F32)
    for copy in range(1, 8):
        packed_ref[copy] = packed_ref[0]


def terms_kernel(source_ref, shares_ref, packed_ref, weight_ref, out_ref, parts_ref, terms_ref):
    flux = jnp.sum(shares_ref[...], axis=0)
    high = flux.astype(jnp.bfloat16).astype(F32)
    rest = flux - high
    middle = rest.astype(jnp.bfloat16).astype(F32)
    parts_ref[...] = jnp.zeros_like(parts_ref)
    parts_ref[:, 0, :] = high
    parts_ref[:, 1, :] = middle
    parts_ref[:, 2, :] = rest - middle
    for t in range(TILES):
        left = parts_ref[source_ref[t]].astype(jnp.bfloat16)
        three = jnp.dot(left, weight_ref[t], preferred_element_type=F32)
        term = jnp.sum(three, axis=0, keepdims=True)
        place = (t + 2 * REACH) % TILES
        while place < TILES + 2 * WINDOW:
            terms_ref[place : place + 1] = term
            place += TILES
    fixed = packed_ref[START : START + 24]
    for p in range(OWNERS):
        out_ref[p, 0:24] = fixed
        out_ref[p, TERMS:SENT] = terms_ref[2 * p : 2 * p + 2 * WINDOW]


def by_distance(left, work):
    work([CENTER])

    def pair(i, carry):
        work([CENTER - i, CENTER + i])
        return carry

    if left:
        lax.fori_loop(1, left + 1, pair, 0)


def load_window(owner_ref, group_ref, staggered_ref, window_ref):
    owner = owner_ref[0]
    for k in range(WINDOW):
        other = (owner + (k - REACH + OWNERS)) % OWNERS
        inside = other // 8 == owner // 8

        @pl.when(inside)
        def _(k=k, other=other):
            window_ref[k] = group_ref[other % 8]

        @pl.when(jnp.logical_not(inside))
        def _(k=k, other=other):
            window_ref[k] = staggered_ref[(other + 4) % 8]


def run_steps(window_ref, lists_ref, forcing_ref, surface_ref, table_ref, scale_ref):
    def spread(left):
        largest = jnp.max(jnp.max(scale_ref[0], axis=1, keepdims=True), axis=0, keepdims=True)
        largest = jnp.maximum(largest, 1e-30)
        scale_ref[1] = jnp.broadcast_to(32767.0 / largest, (8, LANES))
        scale_ref[2] = jnp.broadcast_to(largest * (1.0 / 32767.0), (8, LANES))
        scale_ref[0] = jnp.zeros((8, LANES), F32)

        def work(slots):
            for slot in slots:
                whole = []
                for h in range(2):
                    scaled = surface_ref[slot, 8 * h : 8 * h + 8] * scale_ref[1]
                    whole.append((scaled + jnp.where(scaled < 0, -0.5, 0.5)).astype(I32))
                table_ref[slot, 0:8] = pair_of(*whole)
            sent = []
            for slot in slots:
                value = pick(table_ref.at[slot], 8, lists_ref[slot].astype(I32))
                sent.append(pair_of(value, pltpu.roll(value, 7, 0)))
            for slot, pairs in zip(slots, sent):
                table_ref[slot - 1, 9:10] = pairs[0:1]
                table_ref[slot + 1, 8:9] = pairs[2:3]

        by_distance(left, work)

    def advance(left):
        def work(slots):
            totals = []
            for slot in slots:
                for h in range(2):
                    part = slice(8 * h, 8 * h + 8)
                    flow = None
                    for m in range(6):
                        rows = slice(16 * m + 8 * h, 16 * m + 8 * h + 8)
                        code = window_ref[slot - 2, rows].astype(I32)
                        near = pick(table_ref.at[slot], 10, code).astype(F32)
                        near = window_ref[slot - 2, CONDUCT + 16 * m + 8 * h : CONDUCT + 16 * m + 8 * h + 8] * near
                        flow = near if flow is None else flow + near
                    own = surface_ref[slot, part]
                    keep = window_ref[slot - 2, KEEP + 8 * h : KEEP + 8 * h + 8]
                    totals.append(keep * own + forcing_ref[slot - 2, part] + flow * scale_ref[2])
            largest = scale_ref[0]
            for i, slot in enumerate(slots):
                for h in range(2):
                    total = totals[2 * i + h]
                    surface_ref[slot, 8 * h : 8 * h + 8] = total
                    largest = jnp.maximum(largest, jnp.abs(total))
            scale_ref[0] = largest

        by_distance(left, work)

    largest = jnp.zeros((8, LANES), F32)
    for slot in range(1, WINDOW + 3):
        for h in range(2):
            largest = jnp.maximum(largest, jnp.abs(surface_ref[slot, 8 * h : 8 * h + 8]))
    scale_ref[0] = largest
    spread(REACH + 1)
    for step in range(STEPS):
        left = STEPS - 1 - step
        advance(left)
        if left:
            spread(left)


def first_kernel(owner_ref, arrived_ref, group_ref, staggered_ref, out_ref, lists_ref, forcing_ref, window_ref, terms_ref, surface_ref, table_ref, scale_ref):
    load_window(owner_ref, group_ref, staggered_ref, window_ref)
    owner = owner_ref[0]
    for slot in range(1, WINDOW + 3):
        other = (owner + (slot - CENTER + OWNERS)) % OWNERS
        surface_ref[slot] = arrived_ref[other, 0:16]
        lists_ref[slot] = arrived_ref[other, 16:24]
    for slot in range(1, WINDOW + 3):
        lists_ref[slot, 4:8] = jnp.zeros((4, LANES), F32)
    blocks = lax.broadcasted_iota(I32, (16, TILES), 0)
    for k in range(WINDOW):
        for j in range(2):
            terms_ref[pl.ds(j, OWNERS, stride=2), :] = arrived_ref[:, TERMS + 2 * k + j, :]
        target = window_ref[k, TARGET : TARGET + 1, 0:TILES].astype(I32)
        hot = (blocks == target).astype(F32)
        forcing_ref[k] = jnp.dot(hot, terms_ref[...], precision=HIGHEST, preferred_element_type=F32)
    run_steps(window_ref, lists_ref, forcing_ref, surface_ref, table_ref, scale_ref)
    out_ref[...] = jnp.broadcast_to(surface_ref[CENTER][None], out_ref.shape)


def last_kernel(owner_ref, target_ref, surfaces_ref, group_ref, staggered_ref, lists_ref, forcing_ref, out_ref, values_ref, window_ref, surface_ref, table_ref, scale_ref):
    load_window(owner_ref, group_ref, staggered_ref, window_ref)
    owner = owner_ref[0]
    for slot in range(1, WINDOW + 3):
        surface_ref[slot] = surfaces_ref[(owner + (slot - CENTER + OWNERS)) % OWNERS]
    run_steps(window_ref, lists_ref, forcing_ref, surface_ref, table_ref, scale_ref)
    out_ref[...] = surface_ref[CENTER]
    for t in range(TILES):
        values_ref[t // 2, t % 2 : t % 2 + 1] = surface_ref[CENTER, pl.ds(target_ref[t], 1), :]


def shape(*dims):
    return jax.ShapeDtypeStruct(dims, F32)


def local(
    atm_flux,
    level_weight,
    tile_weight,
    tile_source,
    tile_target,
    ocean_start,
    conductance,
    damping,
    neighbors,
    send_lists,
):
    owner = lax.axis_index("cells").astype(I32).reshape(1)
    window = pltpu.VMEM((WINDOW, PART, LANES), F32)
    scratch = [
        pltpu.VMEM((SLOTS, 16, LANES), F32),
        pltpu.VMEM((SLOTS, 16, LANES), I32),
        pltpu.VMEM((3, 8, LANES), F32),
    ]

    partials, packed = pl.pallas_call(
        prepare_kernel,
        out_shape=(shape(8, 16, LANES), shape(8, PART, LANES)),
        in_specs=[SMEM] + [VMEM] * 7,
        scratch_shapes=[pltpu.VMEM((16, LANES), F32)],
    )(
        level_weight,
        atm_flux,
        neighbors,
        conductance,
        damping.reshape(16, LANES),
        ocean_start.reshape(16, LANES),
        send_lists,
        tile_target.reshape(1, TILES),
    )
    shares = lax.all_to_all(partials, "comp", split_axis=0, concat_axis=0, tiled=True)
    group = exchange(packed, eights(0))
    staggered = exchange(packed, eights(4))
    terms = pl.pallas_call(
        terms_kernel,
        out_shape=shape(OWNERS, SENT, LANES),
        in_specs=[SMEM] + [VMEM] * 3,
        scratch_shapes=[pltpu.VMEM((16, 8, LANES), F32), pltpu.VMEM((TILES + 2 * WINDOW, LANES), F32)],
    )(tile_source, shares, packed[0], tile_weight)
    arrived = exchange(terms, ALL)
    surface, lists, forcing = pl.pallas_call(
        first_kernel,
        out_shape=(shape(OWNERS, 16, LANES), shape(SLOTS, 8, LANES), shape(WINDOW, 16, LANES)),
        in_specs=[SMEM] + [VMEM] * 3,
        scratch_shapes=[window, pltpu.VMEM((TILES, LANES), F32)] + scratch,
    )(owner, arrived, group, staggered)
    surfaces = exchange(surface, ALL)
    ocean_end, values = pl.pallas_call(
        last_kernel,
        out_shape=(shape(16, LANES), shape(OWNERS, 2, LANES)),
        in_specs=[SMEM] * 2 + [VMEM] * 5,
        scratch_shapes=[window] + scratch,
    )(owner, tile_target, surfaces, group, staggered, lists, forcing)
    returned = exchange(values, ALL).reshape(TILES, LANES)
    pulled = jnp.sum(returned[:, None, :] * tile_weight.astype(F32), axis=2)
    source_hot = (tile_source[:, None] == jnp.arange(16, dtype=I32)[None, :]).astype(F32)
    atm_back = jnp.einsum("ra,rb->ab", source_hot, pulled, precision=HIGHEST).reshape(-1)
    return (ocean_end.reshape(-1), atm_back)


def solution(mesh):
    in_specs = (
        P("comp", "cells"),
        P("comp"),
        P("cells", None, None),
        P("cells"),
        P("cells"),
        P("cells"),
        P(None, "cells"),
        P("cells"),
        P(None, "cells"),
        P(None, "cells"),
    )
    out_specs = (P("cells"), P("cells"))
    return jax.shard_map(local, mesh=mesh, in_specs=in_specs, out_specs=out_specs, check_vma=False)
```

```python
import jax
import jax.numpy as jnp
from jax import lax
from jax.experimental import pallas as pl
from jax.experimental.pallas import tpu as pltpu
from jax.sharding import PartitionSpec as P

LANES = 128
OWNERS = 32
HALF = 16
TILES = 64
REACH = 4
STEPS = 5
WINDOW = 2 * REACH + 1
CENTER = REACH + 2
SLOTS = WINDOW + 4
PART = 232
CONDUCT, KEEP, START, LISTS, TARGET = 96, 192, 208, 224, 228
SENT = 40
TERMS = 22
BOTH = ("comp", "cells")
HIGHEST = lax.Precision.HIGHEST
F32, I32 = jnp.float32, jnp.int32
VMEM = pl.BlockSpec(memory_space=pltpu.VMEM)
SMEM = pl.BlockSpec(memory_space=pltpu.SMEM)


def device_of(owner, copy, core):
    z_low = copy if owner < HALF else 3 - copy
    return (2 * z_low + core) * OWNERS + owner


COPIES = [(copy, core) for copy in range(4) for core in range(2)]
ALL = [[device_of(owner, *copy) for owner in range(OWNERS)] for copy in COPIES]


def from_owner(block, offset):
    route = [
        (device_of((owner + offset) % OWNERS, *copy), device_of(owner, *copy))
        for copy in COPIES
        for owner in range(OWNERS)
    ]
    return lax.ppermute(block, BOTH, route)


def exchange(blocks):
    return lax.all_to_all(blocks, BOTH, split_axis=0, concat_axis=0, tiled=True, axis_index_groups=ALL)


def lane_pick(rows, lane):
    dims = lax.GatherDimensionNumbers(
        offset_dims=(),
        collapsed_slice_dims=(1,),
        start_index_map=(1,),
        operand_batching_dims=(0,),
        start_indices_batching_dims=(0,),
    )
    return lax.gather(
        rows,
        lane[..., None],
        dims,
        slice_sizes=(1, 1),
        mode=lax.GatherScatterMode.PROMISE_IN_BOUNDS,
    )


def coded(index):
    row, lane = index >> 7, index & 127
    halo = row >= 16
    pair = jnp.where(halo, 8 + ((row >> 1) & 1), row & 7)
    half = jnp.where(halo, row & 1, row >> 3)
    return pair * 256 + half * 128 + lane


def pair_of(upper, lower):
    return (upper << 16) | (lower & 0xFFFF)


def pick(table_ref, count, code):
    lane, pair = code & 127, code >> 8
    total = None
    for r in range(count):
        line = table_ref[pl.ds(r, 8, stride=0), :]
        near = lane_pick(line, lane)
        total = near if total is None else jnp.where(pair == r, near, total)
    return jnp.where((code & 128) == 0, total, total << 16) >> 16


def prepare_kernel(weight_ref, flux_ref, neighbor_ref, conduct_ref, damping_ref, start_ref, lists_ref, target_ref, shares_ref, packed_ref, row_ref):
    for j in range(16):
        lanes = slice(LANES * j, LANES * j + LANES)
        block = flux_ref[:, lanes].astype(F32)
        row_ref[j : j + 1] = sum(weight_ref[level] * block[level : level + 1] for level in range(block.shape[0]))
    shares_ref[...] = jnp.broadcast_to(row_ref[...][None], shares_ref.shape)
    own = packed_ref
    for j in range(16):
        lanes = slice(LANES * j, LANES * j + LANES)
        own[pl.ds(j, 6, stride=16), :] = coded(neighbor_ref[:, lanes]).astype(F32)
        conduct = conduct_ref[:, lanes]
        own[pl.ds(CONDUCT + j, 6, stride=16), :] = conduct
        own[KEEP + j : KEEP + j + 1] = 1.0 - jnp.sum(conduct, axis=0, keepdims=True) - damping_ref[j : j + 1]
    own[START:LISTS] = start_ref[...]
    for j in range(2):
        lanes = slice(LANES * j, LANES * j + LANES)
        lists = coded(lists_ref[:, lanes]).astype(F32)
        own[LISTS + j : LISTS + j + 1] = lists[0:1]
        own[LISTS + 2 + j : LISTS + 3 + j] = lists[1:2]
    own[TARGET:PART] = jnp.zeros((PART - TARGET, LANES), F32)
    own[TARGET : TARGET + 1, 0:TILES] = target_ref[...].astype(F32)


def terms_kernel(source_ref, shares_ref, packed_ref, weight_ref, out_ref, parts_ref, terms_ref):
    flux = jnp.sum(shares_ref[...], axis=0)
    high = flux.astype(jnp.bfloat16).astype(F32)
    rest = flux - high
    middle = rest.astype(jnp.bfloat16).astype(F32)
    parts_ref[...] = jnp.zeros_like(parts_ref)
    parts_ref[:, 0, :] = high
    parts_ref[:, 1, :] = middle
    parts_ref[:, 2, :] = rest - middle
    for t in range(TILES):
        left = parts_ref[source_ref[t]].astype(jnp.bfloat16)
        three = jnp.dot(left, weight_ref[t], preferred_element_type=F32)
        term = jnp.sum(three, axis=0, keepdims=True)
        place = (t + 2 * REACH) % TILES
        while place < TILES + 2 * WINDOW:
            terms_ref[place : place + 1] = term
            place += TILES
    fixed = packed_ref[START : START + 24]
    for p in range(OWNERS):
        out_ref[p, 0:24] = fixed
        out_ref[p, TERMS:SENT] = terms_ref[2 * p : 2 * p + 2 * WINDOW]


def by_distance(left, work):
    work([CENTER])

    def pair(i, carry):
        work([CENTER - i, CENTER + i])
        return carry

    if left:
        lax.fori_loop(1, left + 1, pair, 0)


def run_steps(window_ref, lists_ref, forcing_ref, surface_ref, table_ref, scale_ref):
    def spread(left):
        largest = jnp.max(jnp.max(scale_ref[0], axis=1, keepdims=True), axis=0, keepdims=True)
        largest = jnp.maximum(largest, 1e-30)
        scale_ref[1] = jnp.broadcast_to(32767.0 / largest, (8, LANES))
        scale_ref[2] = jnp.broadcast_to(largest * (1.0 / 32767.0), (8, LANES))
        scale_ref[0] = jnp.zeros((8, LANES), F32)

        def work(slots):
            for slot in slots:
                whole = []
                for h in range(2):
                    scaled = surface_ref[slot, 8 * h : 8 * h + 8] * scale_ref[1]
                    whole.append((scaled + jnp.where(scaled < 0, -0.5, 0.5)).astype(I32))
                table_ref[slot, 0:8] = pair_of(*whole)
            sent = []
            for slot in slots:
                value = pick(table_ref.at[slot], 8, lists_ref[slot].astype(I32))
                sent.append(pair_of(value, pltpu.roll(value, 7, 0)))
            for slot, pairs in zip(slots, sent):
                table_ref[slot - 1, 9:10] = pairs[0:1]
                table_ref[slot + 1, 8:9] = pairs[2:3]

        by_distance(left, work)

    def advance(left):
        def work(slots):
            totals = []
            for slot in slots:
                for h in range(2):
                    part = slice(8 * h, 8 * h + 8)
                    flow = None
                    for m in range(6):
                        rows = slice(16 * m + 8 * h, 16 * m + 8 * h + 8)
                        code = window_ref[slot - 2, rows].astype(I32)
                        near = pick(table_ref.at[slot], 10, code).astype(F32)
                        near = window_ref[slot - 2, CONDUCT + 16 * m + 8 * h : CONDUCT + 16 * m + 8 * h + 8] * near
                        flow = near if flow is None else flow + near
                    own = surface_ref[slot, part]
                    keep = window_ref[slot - 2, KEEP + 8 * h : KEEP + 8 * h + 8]
                    totals.append(keep * own + forcing_ref[slot - 2, part] + flow * scale_ref[2])
            largest = scale_ref[0]
            for i, slot in enumerate(slots):
                for h in range(2):
                    total = totals[2 * i + h]
                    surface_ref[slot, 8 * h : 8 * h + 8] = total
                    largest = jnp.maximum(largest, jnp.abs(total))
            scale_ref[0] = largest

        by_distance(left, work)

    largest = jnp.zeros((8, LANES), F32)
    for slot in range(1, WINDOW + 3):
        for h in range(2):
            largest = jnp.maximum(largest, jnp.abs(surface_ref[slot, 8 * h : 8 * h + 8]))
    scale_ref[0] = largest
    spread(REACH + 1)
    for step in range(STEPS):
        left = STEPS - 1 - step
        advance(left)
        if left:
            spread(left)


def first_kernel(owner_ref, arrived_ref, window_ref, out_ref, lists_ref, forcing_ref, terms_ref, surface_ref, table_ref, scale_ref):
    owner = owner_ref[0]
    for slot in range(1, WINDOW + 3):
        other = (owner + (slot - CENTER + OWNERS)) % OWNERS
        surface_ref[slot] = arrived_ref[other, 0:16]
        lists_ref[slot] = arrived_ref[other, 16:24]
    for slot in range(1, WINDOW + 3):
        lists_ref[slot, 4:8] = jnp.zeros((4, LANES), F32)
    blocks = lax.broadcasted_iota(I32, (16, TILES), 0)
    for k in range(WINDOW):
        for j in range(2):
            terms_ref[pl.ds(j, OWNERS, stride=2), :] = arrived_ref[:, TERMS + 2 * k + j, :]
        target = window_ref[k, TARGET : TARGET + 1, 0:TILES].astype(I32)
        hot = (blocks == target).astype(F32)
        forcing_ref[k] = jnp.dot(hot, terms_ref[...], precision=HIGHEST, preferred_element_type=F32)
    run_steps(window_ref, lists_ref, forcing_ref, surface_ref, table_ref, scale_ref)
    out_ref[...] = jnp.broadcast_to(surface_ref[CENTER][None], out_ref.shape)


def last_kernel(owner_ref, target_ref, surfaces_ref, window_ref, lists_ref, forcing_ref, out_ref, values_ref, surface_ref, table_ref, scale_ref):
    owner = owner_ref[0]
    for slot in range(1, WINDOW + 3):
        surface_ref[slot] = surfaces_ref[(owner + (slot - CENTER + OWNERS)) % OWNERS]
    run_steps(window_ref, lists_ref, forcing_ref, surface_ref, table_ref, scale_ref)
    out_ref[...] = surface_ref[CENTER]
    for t in range(TILES):
        values_ref[t // 2, t % 2 : t % 2 + 1] = surface_ref[CENTER, pl.ds(target_ref[t], 1), :]


def shape(*dims):
    return jax.ShapeDtypeStruct(dims, F32)


def local(
    atm_flux,
    level_weight,
    tile_weight,
    tile_source,
    tile_target,
    ocean_start,
    conductance,
    damping,
    neighbors,
    send_lists,
):
    owner = lax.axis_index("cells").astype(I32).reshape(1)
    scratch = [
        pltpu.VMEM((SLOTS, 16, LANES), F32),
        pltpu.VMEM((SLOTS, 16, LANES), I32),
        pltpu.VMEM((3, 8, LANES), F32),
    ]

    partials, packed = pl.pallas_call(
        prepare_kernel,
        out_shape=(shape(8, 16, LANES), shape(PART, LANES)),
        in_specs=[SMEM] + [VMEM] * 7,
        scratch_shapes=[pltpu.VMEM((16, LANES), F32)],
    )(
        level_weight,
        atm_flux,
        neighbors,
        conductance,
        damping.reshape(16, LANES),
        ocean_start.reshape(16, LANES),
        send_lists,
        tile_target.reshape(1, TILES),
    )
    with jax.named_scope("levels"):
        shares = lax.all_to_all(partials, "comp", split_axis=0, concat_axis=0, tiled=True)
    with jax.named_scope("near"):
        lower, higher = from_owner(packed, -1), from_owner(packed, 1)
    three = jnp.concatenate([lower, packed, higher], axis=0)
    terms = pl.pallas_call(
        terms_kernel,
        out_shape=shape(OWNERS, SENT, LANES),
        in_specs=[SMEM] + [VMEM] * 3,
        scratch_shapes=[pltpu.VMEM((16, 8, LANES), F32), pltpu.VMEM((TILES + 2 * WINDOW, LANES), F32)],
    )(tile_source, shares, packed, tile_weight)
    with jax.named_scope("send"):
        arrived = exchange(terms)
    with jax.named_scope("far"):
        lower, higher = from_owner(three, -3), from_owner(three, 3)
    window = jnp.concatenate([lower, three, higher], axis=0).reshape(WINDOW, PART, LANES)
    surface, lists, forcing = pl.pallas_call(
        first_kernel,
        out_shape=(shape(OWNERS, 16, LANES), shape(SLOTS, 8, LANES), shape(WINDOW, 16, LANES)),
        in_specs=[SMEM] + [VMEM] * 2,
        scratch_shapes=[pltpu.VMEM((TILES, LANES), F32)] + scratch,
    )(owner, arrived, window)
    surfaces = exchange(surface)
    ocean_end, values = pl.pallas_call(
        last_kernel,
        out_shape=(shape(16, LANES), shape(OWNERS, 2, LANES)),
        in_specs=[SMEM] * 2 + [VMEM] * 4,
        scratch_shapes=scratch,
    )(owner, tile_target, surfaces, window, lists, forcing)
    returned = exchange(values).reshape(TILES, LANES)
    pulled = jnp.sum(returned[:, None, :] * tile_weight.astype(F32), axis=2)
    source_hot = (tile_source[:, None] == jnp.arange(16, dtype=I32)[None, :]).astype(F32)
    atm_back = jnp.einsum("ra,rb->ab", source_hot, pulled, precision=HIGHEST).reshape(-1)
    return (ocean_end.reshape(-1), atm_back)


def solution(mesh):
    in_specs = (
        P("comp", "cells"),
        P("comp"),
        P("cells", None, None),
        P("cells"),
        P("cells"),
        P("cells"),
        P(None, "cells"),
        P("cells"),
        P(None, "cells"),
        P(None, "cells"),
    )
    out_specs = (P("cells"), P("cells"))
    return jax.shard_map(local, mesh=mesh, in_specs=in_specs, out_specs=out_specs, check_vma=False)
```

```python
import jax
import jax.numpy as jnp
from jax import lax
from jax.experimental import pallas as pl
from jax.experimental.pallas import tpu as pltpu
from jax.sharding import PartitionSpec as P

LANES = 128
OWNERS = 32
HALF = 16
TILES = 64
REACH = 4
STEPS = 5
WINDOW = 2 * REACH + 1
CENTER = REACH + 2
SLOTS = WINDOW + 4
PART = 232
CONDUCT, KEEP, START, LISTS, TARGET = 96, 192, 208, 224, 228
SENT = 24
BOTH = ("comp", "cells")
HIGHEST = lax.Precision.HIGHEST
F32, I32 = jnp.float32, jnp.int32
VMEM = pl.BlockSpec(memory_space=pltpu.VMEM)
SMEM = pl.BlockSpec(memory_space=pltpu.SMEM)


def device_of(owner, copy, core):
    z_low = copy if owner < HALF else 3 - copy
    return (2 * z_low + core) * OWNERS + owner


COPIES = [(copy, core) for copy in (0, 3) for core in range(2)]
IDLE = [
    [(2 * z_low + core) * OWNERS + half * HALF + i for core in range(2) for i in range(HALF)]
    for z_low in (1, 2)
    for half in range(2)
]
ALL = [[device_of(owner, *copy) for owner in range(OWNERS)] for copy in COPIES] + IDLE


def from_owner(block, offset):
    route = [
        (device_of((owner + offset) % OWNERS, *copy), device_of(owner, *copy))
        for copy in COPIES
        for owner in range(OWNERS)
    ]
    return lax.ppermute(block, BOTH, route)


def to_idle(block):
    route = [
        ((2 * here + core) * OWNERS + owner, (2 * there + core) * OWNERS + owner)
        for here, there in ((0, 1), (3, 2))
        for core in range(2)
        for owner in range(OWNERS)
    ]
    z_low = lax.axis_index("comp") // 2
    return jnp.where((z_low == 0) | (z_low == 3), block, lax.ppermute(block, BOTH, route))


def exchange(blocks):
    return lax.all_to_all(blocks, BOTH, split_axis=0, concat_axis=0, tiled=True, axis_index_groups=ALL)


def lane_pick(rows, lane):
    dims = lax.GatherDimensionNumbers(
        offset_dims=(),
        collapsed_slice_dims=(1,),
        start_index_map=(1,),
        operand_batching_dims=(0,),
        start_indices_batching_dims=(0,),
    )
    return lax.gather(
        rows,
        lane[..., None],
        dims,
        slice_sizes=(1, 1),
        mode=lax.GatherScatterMode.PROMISE_IN_BOUNDS,
    )


def coded(index):
    row, lane = index >> 7, index & 127
    halo = row >= 16
    pair = jnp.where(halo, 8 + ((row >> 1) & 1), row & 7)
    half = jnp.where(halo, row & 1, row >> 3)
    return pair * 256 + half * 128 + lane


def pair_of(upper, lower):
    return (upper << 16) | (lower & 0xFFFF)


def pick(table_ref, count, code):
    lane, pair = code & 127, code >> 8
    total = None
    for r in range(count):
        line = table_ref[pl.ds(r, 8, stride=0), :]
        near = lane_pick(line, lane)
        total = near if total is None else jnp.where(pair == r, near, total)
    return jnp.where((code & 128) == 0, total, total << 16) >> 16


def prepare_kernel(weight_ref, flux_ref, neighbor_ref, conduct_ref, damping_ref, start_ref, lists_ref, target_ref, shares_ref, packed_ref, row_ref):
    for j in range(16):
        lanes = slice(LANES * j, LANES * j + LANES)
        block = flux_ref[:, lanes].astype(F32)
        row_ref[j : j + 1] = sum(weight_ref[level] * block[level : level + 1] for level in range(block.shape[0]))
    shares_ref[...] = jnp.broadcast_to(row_ref[...][None], shares_ref.shape)
    own = packed_ref
    for j in range(16):
        lanes = slice(LANES * j, LANES * j + LANES)
        own[pl.ds(j, 6, stride=16), :] = coded(neighbor_ref[:, lanes]).astype(F32)
        conduct = conduct_ref[:, lanes]
        own[pl.ds(CONDUCT + j, 6, stride=16), :] = conduct
        own[KEEP + j : KEEP + j + 1] = 1.0 - jnp.sum(conduct, axis=0, keepdims=True) - damping_ref[j : j + 1]
    own[START:LISTS] = start_ref[...]
    for j in range(2):
        lanes = slice(LANES * j, LANES * j + LANES)
        lists = coded(lists_ref[:, lanes]).astype(F32)
        own[LISTS + j : LISTS + j + 1] = lists[0:1]
        own[LISTS + 2 + j : LISTS + 3 + j] = lists[1:2]
    own[TARGET:PART] = jnp.zeros((PART - TARGET, LANES), F32)
    own[TARGET : TARGET + 1, 0:TILES] = target_ref[...].astype(F32)


def terms_kernel(source_ref, shares_ref, weight_ref, out_ref, parts_ref, terms_ref):
    flux = jnp.sum(shares_ref[...], axis=0)
    high = flux.astype(jnp.bfloat16).astype(F32)
    rest = flux - high
    middle = rest.astype(jnp.bfloat16).astype(F32)
    parts_ref[...] = jnp.zeros_like(parts_ref)
    parts_ref[:, 0, :] = high
    parts_ref[:, 1, :] = middle
    parts_ref[:, 2, :] = rest - middle
    for t in range(TILES):
        left = parts_ref[source_ref[t]].astype(jnp.bfloat16)
        three = jnp.dot(left, weight_ref[t], preferred_element_type=F32)
        term = jnp.sum(three, axis=0, keepdims=True)
        place = (t + 2 * REACH) % TILES
        while place < TILES + 2 * WINDOW:
            terms_ref[place : place + 1] = term
            place += TILES
    for p in range(OWNERS):
        out_ref[p, 0 : 2 * WINDOW] = terms_ref[2 * p : 2 * p + 2 * WINDOW]


def by_distance(left, work):
    work([CENTER])

    def pair(i, carry):
        work([CENTER - i, CENTER + i])
        return carry

    if left:
        lax.fori_loop(1, left + 1, pair, 0)


def run_steps(window_ref, lists_ref, forcing_ref, surface_ref, table_ref, scale_ref):
    def spread(left):
        largest = jnp.max(jnp.max(scale_ref[0], axis=1, keepdims=True), axis=0, keepdims=True)
        largest = jnp.maximum(largest, 1e-30)
        scale_ref[1] = jnp.broadcast_to(32767.0 / largest, (8, LANES))
        scale_ref[2] = jnp.broadcast_to(largest * (1.0 / 32767.0), (8, LANES))
        scale_ref[0] = jnp.zeros((8, LANES), F32)

        def work(slots):
            for slot in slots:
                whole = []
                for h in range(2):
                    scaled = surface_ref[slot, 8 * h : 8 * h + 8] * scale_ref[1]
                    whole.append((scaled + jnp.where(scaled < 0, -0.5, 0.5)).astype(I32))
                table_ref[slot, 0:8] = pair_of(*whole)
            sent = []
            for slot in slots:
                value = pick(table_ref.at[slot], 8, lists_ref[slot].astype(I32))
                sent.append(pair_of(value, pltpu.roll(value, 7, 0)))
            for slot, pairs in zip(slots, sent):
                table_ref[slot - 1, 9:10] = pairs[0:1]
                table_ref[slot + 1, 8:9] = pairs[2:3]

        by_distance(left, work)

    def advance(left):
        def work(slots):
            totals = []
            for slot in slots:
                for h in range(2):
                    part = slice(8 * h, 8 * h + 8)
                    flow = None
                    for m in range(6):
                        rows = slice(16 * m + 8 * h, 16 * m + 8 * h + 8)
                        code = window_ref[slot - 2, rows].astype(I32)
                        near = pick(table_ref.at[slot], 10, code).astype(F32)
                        near = window_ref[slot - 2, CONDUCT + 16 * m + 8 * h : CONDUCT + 16 * m + 8 * h + 8] * near
                        flow = near if flow is None else flow + near
                    own = surface_ref[slot, part]
                    keep = window_ref[slot - 2, KEEP + 8 * h : KEEP + 8 * h + 8]
                    totals.append(keep * own + forcing_ref[slot - 2, part] + flow * scale_ref[2])
            largest = scale_ref[0]
            for i, slot in enumerate(slots):
                for h in range(2):
                    total = totals[2 * i + h]
                    surface_ref[slot, 8 * h : 8 * h + 8] = total
                    largest = jnp.maximum(largest, jnp.abs(total))
            scale_ref[0] = largest

        by_distance(left, work)

    largest = jnp.zeros((8, LANES), F32)
    for slot in range(1, WINDOW + 3):
        for h in range(2):
            largest = jnp.maximum(largest, jnp.abs(surface_ref[slot, 8 * h : 8 * h + 8]))
    scale_ref[0] = largest
    spread(REACH + 1)
    for step in range(STEPS):
        left = STEPS - 1 - step
        advance(left)
        if left:
            spread(left)


def first_kernel(arrived_ref, below_ref, above_ref, window_ref, out_ref, lists_ref, forcing_ref, terms_ref, surface_ref, table_ref, scale_ref):
    for slot, ref in ((1, below_ref), (WINDOW + 2, above_ref)):
        surface_ref[slot] = ref[0:16]
        lists_ref[slot] = ref[16:24]
    for slot in range(2, WINDOW + 2):
        surface_ref[slot] = window_ref[slot - 2, START:LISTS]
        lists_ref[slot] = window_ref[slot - 2, LISTS:PART]
    blocks = lax.broadcasted_iota(I32, (16, TILES), 0)
    for k in range(WINDOW):
        for j in range(2):
            terms_ref[pl.ds(j, OWNERS, stride=2), :] = arrived_ref[:, 2 * k + j, :]
        target = window_ref[k, TARGET : TARGET + 1, 0:TILES].astype(I32)
        hot = (blocks == target).astype(F32)
        forcing_ref[k] = jnp.dot(hot, terms_ref[...], precision=HIGHEST, preferred_element_type=F32)
    run_steps(window_ref, lists_ref, forcing_ref, surface_ref, table_ref, scale_ref)
    out_ref[...] = jnp.broadcast_to(surface_ref[CENTER][None], out_ref.shape)


def last_kernel(owner_ref, target_ref, surfaces_ref, window_ref, lists_ref, forcing_ref, out_ref, values_ref, surface_ref, table_ref, scale_ref):
    owner = owner_ref[0]
    for slot in range(1, WINDOW + 3):
        surface_ref[slot] = surfaces_ref[(owner + (slot - CENTER + OWNERS)) % OWNERS]
    run_steps(window_ref, lists_ref, forcing_ref, surface_ref, table_ref, scale_ref)
    out_ref[...] = surface_ref[CENTER]
    for t in range(TILES):
        values_ref[t // 2, t % 2 : t % 2 + 1] = surface_ref[CENTER, pl.ds(target_ref[t], 1), :]


def shape(*dims):
    return jax.ShapeDtypeStruct(dims, F32)


def local(
    atm_flux,
    level_weight,
    tile_weight,
    tile_source,
    tile_target,
    ocean_start,
    conductance,
    damping,
    neighbors,
    send_lists,
):
    owner = lax.axis_index("cells").astype(I32).reshape(1)
    scratch = [
        pltpu.VMEM((SLOTS, 16, LANES), F32),
        pltpu.VMEM((SLOTS, 16, LANES), I32),
        pltpu.VMEM((3, 8, LANES), F32),
    ]

    partials, packed = pl.pallas_call(
        prepare_kernel,
        out_shape=(shape(8, 16, LANES), shape(PART, LANES)),
        in_specs=[SMEM] + [VMEM] * 7,
        scratch_shapes=[pltpu.VMEM((16, LANES), F32)],
    )(
        level_weight,
        atm_flux,
        neighbors,
        conductance,
        damping.reshape(16, LANES),
        ocean_start.reshape(16, LANES),
        send_lists,
        tile_target.reshape(1, TILES),
    )
    with jax.named_scope("levels"):
        shares = lax.all_to_all(partials, "comp", split_axis=0, concat_axis=0, tiled=True)
    with jax.named_scope("near"):
        lower, higher = from_owner(packed, -1), from_owner(packed, 1)
    three = jnp.concatenate([lower, packed, higher], axis=0)
    terms = pl.pallas_call(
        terms_kernel,
        out_shape=shape(OWNERS, SENT, LANES),
        in_specs=[SMEM] + [VMEM] * 2,
        scratch_shapes=[pltpu.VMEM((16, 8, LANES), F32), pltpu.VMEM((TILES + 2 * WINDOW, LANES), F32)],
    )(tile_source, shares, tile_weight)
    with jax.named_scope("send"):
        arrived = exchange(terms)
    with jax.named_scope("far"):
        lower, higher = from_owner(three, -3), from_owner(three, 3)
        outer = packed[START : START + 24]
        below, above = from_owner(outer, -STEPS), from_owner(outer, STEPS)
    window = jnp.concatenate([lower, three, higher], axis=0).reshape(WINDOW, PART, LANES)
    surface, lists, forcing = pl.pallas_call(
        first_kernel,
        out_shape=(shape(OWNERS, 16, LANES), shape(SLOTS, 8, LANES), shape(WINDOW, 16, LANES)),
        scratch_shapes=[pltpu.VMEM((TILES, LANES), F32)] + scratch,
    )(arrived, below, above, window)
    surfaces = exchange(surface)
    ocean_end, values = pl.pallas_call(
        last_kernel,
        out_shape=(shape(16, LANES), shape(OWNERS, 2, LANES)),
        in_specs=[SMEM] * 2 + [VMEM] * 4,
        scratch_shapes=scratch,
    )(owner, tile_target, surfaces, window, lists, forcing)
    ocean_end = to_idle(ocean_end)
    returned = exchange(values).reshape(TILES, LANES)
    pulled = jnp.sum(returned[:, None, :] * tile_weight.astype(F32), axis=2)
    source_hot = (tile_source[:, None] == jnp.arange(16, dtype=I32)[None, :]).astype(F32)
    atm_back = jnp.einsum("ra,rb->ab", source_hot, pulled, precision=HIGHEST).reshape(-1)
    return (ocean_end.reshape(-1), to_idle(atm_back))


def solution(mesh):
    in_specs = (
        P("comp", "cells"),
        P("comp"),
        P("cells", None, None),
        P("cells"),
        P("cells"),
        P("cells"),
        P(None, "cells"),
        P("cells"),
        P(None, "cells"),
        P(None, "cells"),
    )
    out_specs = (P("cells"), P("cells"))
    return jax.shard_map(local, mesh=mesh, in_specs=in_specs, out_specs=out_specs, check_vma=False)
```

```python
import jax
import jax.numpy as jnp
from jax import lax
from jax.experimental import pallas as pl
from jax.experimental.pallas import tpu as pltpu
from jax.sharding import PartitionSpec as P

LANES = 128
OWNERS = 32
HALF = 16
TILES = 64
REACH = 4
STEPS = 5
WINDOW = 2 * REACH + 1
CENTER = REACH + 2
SLOTS = WINDOW + 4
PART = 232
CONDUCT, KEEP, START, LISTS, TARGET = 96, 192, 208, 224, 228
SENT = 40
TERMS = 22
BOTH = ("comp", "cells")
HIGHEST = lax.Precision.HIGHEST
F32, I32 = jnp.float32, jnp.int32
VMEM = pl.BlockSpec(memory_space=pltpu.VMEM)
SMEM = pl.BlockSpec(memory_space=pltpu.SMEM)


def device_of(owner, copy, core):
    z_low = copy if owner < HALF else 3 - copy
    return (2 * z_low + core) * OWNERS + owner


COPIES = [(copy, core) for copy in (0, 3) for core in range(2)]
IDLE = [
    [(2 * z_low + core) * OWNERS + half * HALF + i for core in range(2) for i in range(HALF)]
    for z_low in (1, 2)
    for half in range(2)
]
ALL = [[device_of(owner, *copy) for owner in range(OWNERS)] for copy in COPIES] + IDLE


def from_owner(block, offset):
    route = [
        (device_of((owner + offset) % OWNERS, *copy), device_of(owner, *copy))
        for copy in COPIES
        for owner in range(OWNERS)
    ]
    return lax.ppermute(block, BOTH, route)


def to_idle(block):
    route = [
        ((2 * here + core) * OWNERS + owner, (2 * there + core) * OWNERS + owner)
        for here, there in ((0, 1), (3, 2))
        for core in range(2)
        for owner in range(OWNERS)
    ]
    z_low = lax.axis_index("comp") // 2
    return jnp.where((z_low == 0) | (z_low == 3), block, lax.ppermute(block, BOTH, route))


def exchange(blocks):
    return lax.all_to_all(blocks, BOTH, split_axis=0, concat_axis=0, tiled=True, axis_index_groups=ALL)


def lane_pick(rows, lane):
    dims = lax.GatherDimensionNumbers(
        offset_dims=(),
        collapsed_slice_dims=(1,),
        start_index_map=(1,),
        operand_batching_dims=(0,),
        start_indices_batching_dims=(0,),
    )
    return lax.gather(
        rows,
        lane[..., None],
        dims,
        slice_sizes=(1, 1),
        mode=lax.GatherScatterMode.PROMISE_IN_BOUNDS,
    )


def coded(index):
    row, lane = index >> 7, index & 127
    halo = row >= 16
    pair = jnp.where(halo, 8 + ((row >> 1) & 1), row & 7)
    half = jnp.where(halo, row & 1, row >> 3)
    return pair * 256 + half * 128 + lane


def pair_of(upper, lower):
    return (upper << 16) | (lower & 0xFFFF)


def pick(table_ref, count, code):
    lane, pair = code & 127, code >> 8
    total = None
    for r in range(count):
        line = table_ref[pl.ds(r, 8, stride=0), :]
        near = lane_pick(line, lane)
        total = near if total is None else jnp.where(pair == r, near, total)
    return jnp.where((code & 128) == 0, total, total << 16) >> 16


def prepare_kernel(weight_ref, flux_ref, neighbor_ref, conduct_ref, damping_ref, start_ref, lists_ref, target_ref, shares_ref, packed_ref, row_ref):
    for j in range(16):
        lanes = slice(LANES * j, LANES * j + LANES)
        block = flux_ref[:, lanes].astype(F32)
        row_ref[j : j + 1] = sum(weight_ref[level] * block[level : level + 1] for level in range(block.shape[0]))
    shares_ref[...] = jnp.broadcast_to(row_ref[...][None], shares_ref.shape)
    own = packed_ref
    for j in range(16):
        lanes = slice(LANES * j, LANES * j + LANES)
        own[pl.ds(j, 6, stride=16), :] = coded(neighbor_ref[:, lanes]).astype(F32)
        conduct = conduct_ref[:, lanes]
        own[pl.ds(CONDUCT + j, 6, stride=16), :] = conduct
        own[KEEP + j : KEEP + j + 1] = 1.0 - jnp.sum(conduct, axis=0, keepdims=True) - damping_ref[j : j + 1]
    own[START:LISTS] = start_ref[...]
    for j in range(2):
        lanes = slice(LANES * j, LANES * j + LANES)
        lists = coded(lists_ref[:, lanes]).astype(F32)
        own[LISTS + j : LISTS + j + 1] = lists[0:1]
        own[LISTS + 2 + j : LISTS + 3 + j] = lists[1:2]
    own[TARGET:PART] = jnp.zeros((PART - TARGET, LANES), F32)
    own[TARGET : TARGET + 1, 0:TILES] = target_ref[...].astype(F32)


def terms_kernel(source_ref, shares_ref, packed_ref, weight_ref, out_ref, parts_ref, terms_ref):
    flux = jnp.sum(shares_ref[...], axis=0)
    high = flux.astype(jnp.bfloat16).astype(F32)
    rest = flux - high
    middle = rest.astype(jnp.bfloat16).astype(F32)
    parts_ref[...] = jnp.zeros_like(parts_ref)
    parts_ref[:, 0, :] = high
    parts_ref[:, 1, :] = middle
    parts_ref[:, 2, :] = rest - middle
    for t in range(TILES):
        left = parts_ref[source_ref[t]].astype(jnp.bfloat16)
        three = jnp.dot(left, weight_ref[t], preferred_element_type=F32)
        term = jnp.sum(three, axis=0, keepdims=True)
        place = (t + 2 * REACH) % TILES
        while place < TILES + 2 * WINDOW:
            terms_ref[place : place + 1] = term
            place += TILES
    fixed = packed_ref[START : START + 24]
    for p in range(OWNERS):
        out_ref[p, 0:24] = fixed
        out_ref[p, TERMS:SENT] = terms_ref[2 * p : 2 * p + 2 * WINDOW]


def by_distance(left, work):
    work([CENTER])

    def pair(i, carry):
        work([CENTER - i, CENTER + i])
        return carry

    if left:
        lax.fori_loop(1, left + 1, pair, 0)


def run_steps(window_ref, lists_ref, forcing_ref, surface_ref, table_ref, scale_ref):
    def spread(left):
        largest = jnp.max(jnp.max(scale_ref[0], axis=1, keepdims=True), axis=0, keepdims=True)
        largest = jnp.maximum(largest, 1e-30)
        scale_ref[1] = jnp.broadcast_to(32767.0 / largest, (8, LANES))
        scale_ref[2] = jnp.broadcast_to(largest * (1.0 / 32767.0), (8, LANES))
        scale_ref[0] = jnp.zeros((8, LANES), F32)

        def work(slots):
            for slot in slots:
                whole = []
                for h in range(2):
                    scaled = surface_ref[slot, 8 * h : 8 * h + 8] * scale_ref[1]
                    whole.append((scaled + jnp.where(scaled < 0, -0.5, 0.5)).astype(I32))
                table_ref[slot, 0:8] = pair_of(*whole)
            sent = []
            for slot in slots:
                value = pick(table_ref.at[slot], 8, lists_ref[slot].astype(I32))
                sent.append(pair_of(value, pltpu.roll(value, 7, 0)))
            for slot, pairs in zip(slots, sent):
                table_ref[slot - 1, 9:10] = pairs[0:1]
                table_ref[slot + 1, 8:9] = pairs[2:3]

        by_distance(left, work)

    def advance(left):
        def work(slots):
            totals = []
            for slot in slots:
                for h in range(2):
                    part = slice(8 * h, 8 * h + 8)
                    flow = None
                    for m in range(6):
                        rows = slice(16 * m + 8 * h, 16 * m + 8 * h + 8)
                        code = window_ref[slot - 2, rows].astype(I32)
                        near = pick(table_ref.at[slot], 10, code).astype(F32)
                        near = window_ref[slot - 2, CONDUCT + 16 * m + 8 * h : CONDUCT + 16 * m + 8 * h + 8] * near
                        flow = near if flow is None else flow + near
                    own = surface_ref[slot, part]
                    keep = window_ref[slot - 2, KEEP + 8 * h : KEEP + 8 * h + 8]
                    totals.append(keep * own + forcing_ref[slot - 2, part] + flow * scale_ref[2])
            largest = scale_ref[0]
            for i, slot in enumerate(slots):
                for h in range(2):
                    total = totals[2 * i + h]
                    surface_ref[slot, 8 * h : 8 * h + 8] = total
                    largest = jnp.maximum(largest, jnp.abs(total))
            scale_ref[0] = largest

        by_distance(left, work)

    largest = jnp.zeros((8, LANES), F32)
    for slot in range(1, WINDOW + 3):
        for h in range(2):
            largest = jnp.maximum(largest, jnp.abs(surface_ref[slot, 8 * h : 8 * h + 8]))
    scale_ref[0] = largest
    spread(REACH + 1)
    for step in range(STEPS):
        left = STEPS - 1 - step
        advance(left)
        if left:
            spread(left)


def first_kernel(owner_ref, arrived_ref, window_ref, out_ref, lists_ref, forcing_ref, terms_ref, surface_ref, table_ref, scale_ref):
    owner = owner_ref[0]
    for slot in range(1, WINDOW + 3):
        other = (owner + (slot - CENTER + OWNERS)) % OWNERS
        surface_ref[slot] = arrived_ref[other, 0:16]
        lists_ref[slot] = arrived_ref[other, 16:24]
    for slot in range(1, WINDOW + 3):
        lists_ref[slot, 4:8] = jnp.zeros((4, LANES), F32)
    blocks = lax.broadcasted_iota(I32, (16, TILES), 0)
    for k in range(WINDOW):
        for j in range(2):
            terms_ref[pl.ds(j, OWNERS, stride=2), :] = arrived_ref[:, TERMS + 2 * k + j, :]
        target = window_ref[k, TARGET : TARGET + 1, 0:TILES].astype(I32)
        hot = (blocks == target).astype(F32)
        forcing_ref[k] = jnp.dot(hot, terms_ref[...], precision=HIGHEST, preferred_element_type=F32)
    run_steps(window_ref, lists_ref, forcing_ref, surface_ref, table_ref, scale_ref)
    out_ref[...] = jnp.broadcast_to(surface_ref[CENTER][None], out_ref.shape)


def last_kernel(owner_ref, target_ref, surfaces_ref, window_ref, lists_ref, forcing_ref, out_ref, values_ref, surface_ref, table_ref, scale_ref):
    owner = owner_ref[0]
    for slot in range(1, WINDOW + 3):
        surface_ref[slot] = surfaces_ref[(owner + (slot - CENTER + OWNERS)) % OWNERS]
    run_steps(window_ref, lists_ref, forcing_ref, surface_ref, table_ref, scale_ref)
    out_ref[...] = surface_ref[CENTER]
    for t in range(TILES):
        values_ref[t // 2, t % 2 : t % 2 + 1] = surface_ref[CENTER, pl.ds(target_ref[t], 1), :]


def shape(*dims):
    return jax.ShapeDtypeStruct(dims, F32)


def local(
    atm_flux,
    level_weight,
    tile_weight,
    tile_source,
    tile_target,
    ocean_start,
    conductance,
    damping,
    neighbors,
    send_lists,
):
    owner = lax.axis_index("cells").astype(I32).reshape(1)
    scratch = [
        pltpu.VMEM((SLOTS, 16, LANES), F32),
        pltpu.VMEM((SLOTS, 16, LANES), I32),
        pltpu.VMEM((3, 8, LANES), F32),
    ]

    partials, packed = pl.pallas_call(
        prepare_kernel,
        out_shape=(shape(8, 16, LANES), shape(PART, LANES)),
        in_specs=[SMEM] + [VMEM] * 7,
        scratch_shapes=[pltpu.VMEM((16, LANES), F32)],
    )(
        level_weight,
        atm_flux,
        neighbors,
        conductance,
        damping.reshape(16, LANES),
        ocean_start.reshape(16, LANES),
        send_lists,
        tile_target.reshape(1, TILES),
    )
    with jax.named_scope("levels"):
        shares = lax.all_to_all(partials, "comp", split_axis=0, concat_axis=0, tiled=True)
    with jax.named_scope("near"):
        lower, higher = from_owner(packed, -1), from_owner(packed, 1)
    three = jnp.concatenate([lower, packed, higher], axis=0)
    terms = pl.pallas_call(
        terms_kernel,
        out_shape=shape(OWNERS, SENT, LANES),
        in_specs=[SMEM] + [VMEM] * 3,
        scratch_shapes=[pltpu.VMEM((16, 8, LANES), F32), pltpu.VMEM((TILES + 2 * WINDOW, LANES), F32)],
    )(tile_source, shares, packed, tile_weight)
    with jax.named_scope("send"):
        arrived = exchange(terms)
    with jax.named_scope("far"):
        lower, higher = from_owner(three, -3), from_owner(three, 3)
    window = jnp.concatenate([lower, three, higher], axis=0).reshape(WINDOW, PART, LANES)
    surface, lists, forcing = pl.pallas_call(
        first_kernel,
        out_shape=(shape(OWNERS, 16, LANES), shape(SLOTS, 8, LANES), shape(WINDOW, 16, LANES)),
        in_specs=[SMEM] + [VMEM] * 2,
        scratch_shapes=[pltpu.VMEM((TILES, LANES), F32)] + scratch,
    )(owner, arrived, window)
    surfaces = exchange(surface)
    ocean_end, values = pl.pallas_call(
        last_kernel,
        out_shape=(shape(16, LANES), shape(OWNERS, 2, LANES)),
        in_specs=[SMEM] * 2 + [VMEM] * 4,
        scratch_shapes=scratch,
    )(owner, tile_target, surfaces, window, lists, forcing)
    ocean_end = to_idle(ocean_end)
    returned = exchange(values).reshape(TILES, LANES)
    pulled = jnp.sum(returned[:, None, :] * tile_weight.astype(F32), axis=2)
    source_hot = (tile_source[:, None] == jnp.arange(16, dtype=I32)[None, :]).astype(F32)
    atm_back = jnp.einsum("ra,rb->ab", source_hot, pulled, precision=HIGHEST).reshape(-1)
    return (ocean_end.reshape(-1), to_idle(atm_back))


def solution(mesh):
    in_specs = (
        P("comp", "cells"),
        P("comp"),
        P("cells", None, None),
        P("cells"),
        P("cells"),
        P("cells"),
        P(None, "cells"),
        P("cells"),
        P(None, "cells"),
        P(None, "cells"),
    )
    out_specs = (P("cells"), P("cells"))
    return jax.shard_map(local, mesh=mesh, in_specs=in_specs, out_specs=out_specs, check_vma=False)
```

```python
import jax
import jax.numpy as jnp
from jax import lax
from jax.experimental import pallas as pl
from jax.experimental.pallas import tpu as pltpu
from jax.sharding import PartitionSpec as P


LANES = 128
OWNERS = 32
HALF = 16
TILES = 64
REACH = 4
STEPS = 5
WINDOW = 2 * REACH + 1
CENTER = REACH + 2
SLOTS = WINDOW + 4
PART = 232
CONDUCT, KEEP, START, LISTS, TARGET = 96, 192, 208, 224, 228
SENT = 40
TERMS = 22
BOTH = ("comp", "cells")
HIGHEST = lax.Precision.HIGHEST
F32, I32 = jnp.float32, jnp.int32
VMEM = pl.BlockSpec(memory_space=pltpu.VMEM)
SMEM = pl.BlockSpec(memory_space=pltpu.SMEM)


def device_of(owner, copy, core):
    z_low = copy if owner < HALF else 3 - copy
    return (2 * z_low + core) * OWNERS + owner


COPIES = [(copy, core) for copy in (0, 3) for core in range(2)]
IDLE = [
    [(2 * z_low + core) * OWNERS + half * HALF + i for core in range(2) for i in range(HALF)]
    for z_low in (1, 2)
    for half in range(2)
]
ALL = [[device_of(owner, *copy) for owner in range(OWNERS)] for copy in COPIES] + IDLE


def from_owner(block, offset):
    route = [
        (device_of((owner + offset) % OWNERS, *copy), device_of(owner, *copy))
        for copy in COPIES
        for owner in range(OWNERS)
    ]
    return lax.ppermute(block, BOTH, route)


def to_idle(block):
    route = [
        ((2 * here + core) * OWNERS + owner, (2 * there + core) * OWNERS + owner)
        for here, there in ((0, 1), (3, 2))
        for core in range(2)
        for owner in range(OWNERS)
    ]
    z_low = lax.axis_index("comp") // 2
    return jnp.where((z_low == 0) | (z_low == 3), block, lax.ppermute(block, BOTH, route))


def exchange(blocks):
    return lax.all_to_all(blocks, BOTH, split_axis=0, concat_axis=0, tiled=True, axis_index_groups=ALL)


def lane_pick(rows, lane):
    dims = lax.GatherDimensionNumbers(
        offset_dims=(),
        collapsed_slice_dims=(1,),
        start_index_map=(1,),
        operand_batching_dims=(0,),
        start_indices_batching_dims=(0,),
    )
    return lax.gather(
        rows,
        lane[..., None],
        dims,
        slice_sizes=(1, 1),
        mode=lax.GatherScatterMode.PROMISE_IN_BOUNDS,
    )


def coded(index):
    row, lane = index >> 7, index & 127
    halo = row >= 16
    pair = jnp.where(halo, 8 + ((row >> 1) & 1), row & 7)
    half = jnp.where(halo, row & 1, row >> 3)
    return pair * 256 + half * 128 + lane


def pair_of(upper, lower):
    return (upper << 16) | (lower & 0xFFFF)


def pick(table_ref, count, code):
    lane, pair = code & 127, code >> 8
    total = None
    for r in range(count):
        line = table_ref[pl.ds(r, 8, stride=0), :]
        near = lane_pick(line, lane)
        total = near if total is None else jnp.where(pair == r, near, total)
    return jnp.where((code & 128) == 0, total, total << 16) >> 16


def prepare_kernel(weight_ref, flux_ref, neighbor_ref, conduct_ref, damping_ref, start_ref, lists_ref, target_ref, shares_ref, packed_ref, row_ref):
    for j in range(16):
        lanes = slice(LANES * j, LANES * j + LANES)
        block = flux_ref[:, lanes].astype(F32)
        row_ref[j : j + 1] = sum(weight_ref[level] * block[level : level + 1] for level in range(block.shape[0]))
    shares_ref[...] = jnp.broadcast_to(row_ref[...][None], shares_ref.shape)
    own = packed_ref
    for j in range(16):
        lanes = slice(LANES * j, LANES * j + LANES)
        own[pl.ds(j, 6, stride=16), :] = coded(neighbor_ref[:, lanes]).astype(F32)
        conduct = conduct_ref[:, lanes]
        own[pl.ds(CONDUCT + j, 6, stride=16), :] = conduct
        own[KEEP + j : KEEP + j + 1] = 1.0 - jnp.sum(conduct, axis=0, keepdims=True) - damping_ref[j : j + 1]
    own[START:LISTS] = start_ref[...]
    for j in range(2):
        lanes = slice(LANES * j, LANES * j + LANES)
        lists = coded(lists_ref[:, lanes]).astype(F32)
        own[LISTS + j : LISTS + j + 1] = lists[0:1]
        own[LISTS + 2 + j : LISTS + 3 + j] = lists[1:2]
    own[TARGET:PART] = jnp.zeros((PART - TARGET, LANES), F32)
    own[TARGET : TARGET + 1, 0:TILES] = target_ref[...].astype(F32)


def terms_kernel(source_ref, shares_ref, packed_ref, weight_ref, out_ref, parts_ref, terms_ref):
    flux = jnp.sum(shares_ref[...], axis=0)
    high = flux.astype(jnp.bfloat16).astype(F32)
    rest = flux - high
    middle = rest.astype(jnp.bfloat16).astype(F32)
    parts_ref[...] = jnp.zeros_like(parts_ref)
    parts_ref[:, 0, :] = high
    parts_ref[:, 1, :] = middle
    parts_ref[:, 2, :] = rest - middle
    for t in range(TILES):
        left = parts_ref[source_ref[t]].astype(jnp.bfloat16)
        three = jnp.dot(left, weight_ref[t], preferred_element_type=F32)
        term = jnp.sum(three, axis=0, keepdims=True)
        place = (t + 2 * REACH) % TILES
        while place < TILES + 2 * WINDOW:
            terms_ref[place : place + 1] = term
            place += TILES
    fixed = packed_ref[START : START + 24]
    for p in range(OWNERS):
        out_ref[p, 0:24] = fixed
        out_ref[p, TERMS:SENT] = terms_ref[2 * p : 2 * p + 2 * WINDOW]


def groups(left):
    if left == 0:
        return [[CENTER]]
    pairs = [[CENTER - i, CENTER + i] for i in range(2, left + 1)]
    return [[CENTER, CENTER - 1, CENTER + 1]] + pairs


def run_steps(parts, lists_ref, forcing_ref, surface_ref, table_ref):
    def part(slot):
        return parts[(slot - 2) // 3].at[(slot - 2) % 3]

    def spread(left, largest):
        largest = jnp.max(jnp.max(largest, axis=1, keepdims=True), axis=0, keepdims=True)
        largest = jnp.maximum(largest, 1e-30)
        scale = jnp.broadcast_to(32767.0 / largest, (8, LANES))
        slots = range(CENTER - left, CENTER + left + 1)
        for slot in slots:
            whole = []
            for h in range(2):
                scaled = surface_ref[slot, 8 * h : 8 * h + 8] * scale
                whole.append((scaled + jnp.where(scaled < 0, -0.5, 0.5)).astype(I32))
            table_ref[slot, 0:8] = pair_of(*whole)
        for slot in slots:
            value = pick(table_ref.at[slot], 8, lists_ref[slot].astype(I32))
            pairs = pair_of(value, pltpu.roll(value, 7, 0))
            table_ref[slot - 1, 9:10] = pairs[0:1]
            table_ref[slot + 1, 8:9] = pairs[2:3]
        return jnp.broadcast_to(largest * (1.0 / 32767.0), (8, LANES))

    def advance(left, unit):
        largest = jnp.zeros((8, LANES), F32)
        for slots in groups(left):
            for slot in slots:
                own_part = part(slot)
                for h in range(2):
                    rows = slice(8 * h, 8 * h + 8)
                    flow = None
                    for m in range(6):
                        first = 16 * m + 8 * h
                        near = pick(table_ref.at[slot], 10, own_part[first : first + 8].astype(I32)).astype(F32)
                        near = own_part[CONDUCT + first : CONDUCT + first + 8] * near
                        flow = near if flow is None else flow + near
                    keep = own_part[KEEP + 8 * h : KEEP + 8 * h + 8]
                    total = keep * surface_ref[slot, rows] + forcing_ref[slot - 2, rows] + flow * unit
                    surface_ref[slot, rows] = total
                    largest = jnp.maximum(largest, jnp.abs(total))
        return largest

    largest = jnp.zeros((8, LANES), F32)
    for slot in range(1, WINDOW + 3):
        for h in range(2):
            largest = jnp.maximum(largest, jnp.abs(surface_ref[slot, 8 * h : 8 * h + 8]))
    unit = spread(REACH + 1, largest)
    for left in reversed(range(STEPS)):
        largest = advance(left, unit)
        if left:
            unit = spread(left, largest)


def first_kernel(owner_ref, arrived_ref, low_ref, middle_ref, high_ref, out_ref, lists_ref, forcing_ref, terms_ref, surface_ref, table_ref):
    parts = (low_ref, middle_ref, high_ref)
    owner = owner_ref[0]
    for slot in range(1, WINDOW + 3):
        other = (owner + (slot - CENTER + OWNERS)) % OWNERS
        surface_ref[slot] = arrived_ref[other, 0:16]
        lists_ref[slot] = arrived_ref[other, 16:24]
    for slot in range(1, WINDOW + 3):
        lists_ref[slot, 4:8] = jnp.zeros((4, LANES), F32)
    blocks = lax.broadcasted_iota(I32, (16, TILES), 0)
    for k in range(WINDOW):
        for j in range(2):
            terms_ref[pl.ds(j, OWNERS, stride=2), :] = arrived_ref[:, TERMS + 2 * k + j, :]
        target = parts[k // 3][k % 3, TARGET : TARGET + 1, 0:TILES].astype(I32)
        hot = (blocks == target).astype(F32)
        forcing_ref[k] = jnp.dot(hot, terms_ref[...], precision=HIGHEST, preferred_element_type=F32)
    run_steps(parts, lists_ref, forcing_ref, surface_ref, table_ref)
    out_ref[...] = jnp.broadcast_to(surface_ref[CENTER][None], out_ref.shape)


def last_kernel(owner_ref, target_ref, surfaces_ref, low_ref, middle_ref, high_ref, lists_ref, forcing_ref, out_ref, values_ref, surface_ref, table_ref):
    parts = (low_ref, middle_ref, high_ref)
    owner = owner_ref[0]
    for slot in range(1, WINDOW + 3):
        surface_ref[slot] = surfaces_ref[(owner + (slot - CENTER + OWNERS)) % OWNERS]
    run_steps(parts, lists_ref, forcing_ref, surface_ref, table_ref)
    out_ref[...] = surface_ref[CENTER]
    for t in range(TILES):
        values_ref[t // 2, t % 2 : t % 2 + 1] = surface_ref[CENTER, pl.ds(target_ref[t], 1), :]


def shape(*dims):
    return jax.ShapeDtypeStruct(dims, F32)


def local(
    atm_flux,
    level_weight,
    tile_weight,
    tile_source,
    tile_target,
    ocean_start,
    conductance,
    damping,
    neighbors,
    send_lists,
):
    owner = lax.axis_index("cells").astype(I32).reshape(1)
    scratch = [
        pltpu.VMEM((SLOTS, 16, LANES), F32),
        pltpu.VMEM((SLOTS, 16, LANES), I32),
    ]

    partials, packed = pl.pallas_call(
        prepare_kernel,
        out_shape=(shape(8, 16, LANES), shape(PART, LANES)),
        in_specs=[SMEM] + [VMEM] * 7,
        scratch_shapes=[pltpu.VMEM((16, LANES), F32)],
    )(
        level_weight,
        atm_flux,
        neighbors,
        conductance,
        damping.reshape(16, LANES),
        ocean_start.reshape(16, LANES),
        send_lists,
        tile_target.reshape(1, TILES),
    )
    shares = lax.all_to_all(partials, "comp", split_axis=0, concat_axis=0, tiled=True)
    lower, higher = from_owner(packed, -1), from_owner(packed, 1)
    three = jnp.concatenate([lower, packed, higher], axis=0)
    terms = pl.pallas_call(
        terms_kernel,
        out_shape=shape(OWNERS, SENT, LANES),
        in_specs=[SMEM] + [VMEM] * 3,
        scratch_shapes=[pltpu.VMEM((16, 8, LANES), F32), pltpu.VMEM((TILES + 2 * WINDOW, LANES), F32)],
    )(tile_source, shares, packed, tile_weight)
    arrived = exchange(terms)
    lower, higher = from_owner(three, -3), from_owner(three, 3)
    window = [block.reshape(3, PART, LANES) for block in (lower, three, higher)]
    surface, lists, forcing = pl.pallas_call(
        first_kernel,
        out_shape=(shape(OWNERS, 16, LANES), shape(SLOTS, 8, LANES), shape(WINDOW, 16, LANES)),
        in_specs=[SMEM] + [VMEM] * 4,
        scratch_shapes=[pltpu.VMEM((TILES, LANES), F32)] + scratch,
    )(owner, arrived, *window)
    surfaces = exchange(surface)
    ocean_end, values = pl.pallas_call(
        last_kernel,
        out_shape=(shape(16, LANES), shape(OWNERS, 2, LANES)),
        in_specs=[SMEM] * 2 + [VMEM] * 6,
        scratch_shapes=scratch,
    )(owner, tile_target, surfaces, *window, lists, forcing)
    ocean_end = to_idle(ocean_end)
    returned = exchange(values).reshape(TILES, LANES)
    pulled = jnp.sum(returned[:, None, :] * tile_weight.astype(F32), axis=2)
    source_hot = (tile_source[:, None] == jnp.arange(16, dtype=I32)[None, :]).astype(F32)
    atm_back = jnp.einsum("ra,rb->ab", source_hot, pulled, precision=HIGHEST).reshape(-1)
    return (ocean_end.reshape(-1), to_idle(atm_back))


def solution(mesh):
    in_specs = (
        P("comp", "cells"),
        P("comp"),
        P("cells", None, None),
        P("cells"),
        P("cells"),
        P("cells"),
        P(None, "cells"),
        P("cells"),
        P(None, "cells"),
        P(None, "cells"),
    )
    out_specs = (P("cells"), P("cells"))
    return jax.shard_map(local, mesh=mesh, in_specs=in_specs, out_specs=out_specs, check_vma=False)
```

```python
import jax
import jax.numpy as jnp
from jax import lax
from jax.experimental import pallas as pl
from jax.experimental.pallas import tpu as pltpu
from jax.sharding import PartitionSpec as P


LANES = 128
OWNERS = 32
HALF = 16
TILES = 64
REACH = 4
STEPS = 5
WINDOW = 2 * REACH + 1
CENTER = REACH + 2
SLOTS = WINDOW + 4
PART = 232
CONDUCT, KEEP, START, LISTS, TARGET = 96, 192, 208, 224, 228
SENT = 40
TERMS = 22
BOTH = ("comp", "cells")
HIGHEST = lax.Precision.HIGHEST
F32, I32 = jnp.float32, jnp.int32
VMEM = pl.BlockSpec(memory_space=pltpu.VMEM)
SMEM = pl.BlockSpec(memory_space=pltpu.SMEM)


def device_of(owner, copy, core):
    z_low = copy if owner < HALF else 3 - copy
    return (2 * z_low + core) * OWNERS + owner


COPIES = [(0, 0), (3, 0)]
PLANES = [[(1, 0), (1, 1)], [(2, 0), (2, 1)], [(0, 1), (3, 1)]]
IDLE = [
    [(2 * z_low + core) * OWNERS + half * HALF + i for z_low, core in planes for i in range(HALF)]
    for planes in PLANES
    for half in range(2)
]
ALL = [[device_of(owner, *copy) for owner in range(OWNERS)] for copy in COPIES] + IDLE


def from_owner(block, offset):
    route = [
        (device_of((owner + offset) % OWNERS, *copy), device_of(owner, *copy))
        for copy in COPIES
        for owner in range(OWNERS)
    ]
    return lax.ppermute(block, BOTH, route)


def to_idle(block):
    arrived = []
    for aside, core in ((1, 0), (1, 1), (0, 1)):
        route = [
            (2 * here * OWNERS + owner, (2 * (there if aside else here) + core) * OWNERS + owner)
            for here, there in ((0, 1), (3, 2))
            for owner in range(OWNERS)
        ]
        arrived.append(lax.ppermute(block, BOTH, route))
    seat = lax.axis_index("comp")
    return jnp.where((seat == 0) | (seat == 6), block, arrived[0] + arrived[1] + arrived[2])


def exchange(blocks):
    return lax.all_to_all(blocks, BOTH, split_axis=0, concat_axis=0, tiled=True, axis_index_groups=ALL)


def lane_pick(rows, lane):
    dims = lax.GatherDimensionNumbers(
        offset_dims=(),
        collapsed_slice_dims=(1,),
        start_index_map=(1,),
        operand_batching_dims=(0,),
        start_indices_batching_dims=(0,),
    )
    return lax.gather(
        rows,
        lane[..., None],
        dims,
        slice_sizes=(1, 1),
        mode=lax.GatherScatterMode.PROMISE_IN_BOUNDS,
    )


def coded(index):
    row, lane = index >> 7, index & 127
    halo = row >= 16
    pair = jnp.where(halo, 8 + ((row >> 1) & 1), row & 7)
    half = jnp.where(halo, row & 1, row >> 3)
    return pair * 256 + half * 128 + lane


def pair_of(upper, lower):
    return (upper << 16) | (lower & 0xFFFF)


def pick(table_ref, count, code):
    lane, pair = code & 127, code >> 8
    total = None
    for r in range(count):
        line = table_ref[pl.ds(r, 8, stride=0), :]
        near = lane_pick(line, lane)
        total = near if total is None else jnp.where(pair == r, near, total)
    return jnp.where((code & 128) == 0, total, total << 16) >> 16


def prepare_kernel(weight_ref, flux_ref, neighbor_ref, conduct_ref, damping_ref, start_ref, lists_ref, target_ref, shares_ref, packed_ref, row_ref):
    for j in range(16):
        lanes = slice(LANES * j, LANES * j + LANES)
        block = flux_ref[:, lanes].astype(F32)
        row_ref[j : j + 1] = sum(weight_ref[level] * block[level : level + 1] for level in range(block.shape[0]))
    shares_ref[...] = jnp.broadcast_to(row_ref[...][None], shares_ref.shape)
    own = packed_ref
    for j in range(16):
        lanes = slice(LANES * j, LANES * j + LANES)
        own[pl.ds(j, 6, stride=16), :] = coded(neighbor_ref[:, lanes]).astype(F32)
        conduct = conduct_ref[:, lanes]
        own[pl.ds(CONDUCT + j, 6, stride=16), :] = conduct
        own[KEEP + j : KEEP + j + 1] = 1.0 - jnp.sum(conduct, axis=0, keepdims=True) - damping_ref[j : j + 1]
    own[START:LISTS] = start_ref[...]
    for j in range(2):
        lanes = slice(LANES * j, LANES * j + LANES)
        lists = coded(lists_ref[:, lanes]).astype(F32)
        own[LISTS + j : LISTS + j + 1] = lists[0:1]
        own[LISTS + 2 + j : LISTS + 3 + j] = lists[1:2]
    own[TARGET:PART] = jnp.zeros((PART - TARGET, LANES), F32)
    own[TARGET : TARGET + 1, 0:TILES] = target_ref[...].astype(F32)


def terms_kernel(source_ref, shares_ref, packed_ref, weight_ref, out_ref, parts_ref, terms_ref):
    flux = jnp.sum(shares_ref[...], axis=0)
    high = flux.astype(jnp.bfloat16).astype(F32)
    rest = flux - high
    middle = rest.astype(jnp.bfloat16).astype(F32)
    parts_ref[...] = jnp.zeros_like(parts_ref)
    parts_ref[:, 0, :] = high
    parts_ref[:, 1, :] = middle
    parts_ref[:, 2, :] = rest - middle
    for t in range(TILES):
        left = parts_ref[source_ref[t]].astype(jnp.bfloat16)
        three = jnp.dot(left, weight_ref[t], preferred_element_type=F32)
        term = jnp.sum(three, axis=0, keepdims=True)
        place = (t + 2 * REACH) % TILES
        while place < TILES + 2 * WINDOW:
            terms_ref[place : place + 1] = term
            place += TILES
    fixed = packed_ref[START : START + 24]
    for p in range(OWNERS):
        out_ref[p, 0:24] = fixed
        out_ref[p, TERMS:SENT] = terms_ref[2 * p : 2 * p + 2 * WINDOW]


def groups(left):
    if left == 0:
        return [[CENTER]]
    pairs = [[CENTER - i, CENTER + i] for i in range(2, left + 1)]
    return [[CENTER, CENTER - 1, CENTER + 1]] + pairs


def run_steps(parts, lists_ref, forcing_ref, surface_ref, table_ref):
    def part(slot):
        return parts[(slot - 2) % 3].at[(slot - 2) // 3]

    def spread(left, largest):
        largest = jnp.max(jnp.max(largest, axis=1, keepdims=True), axis=0, keepdims=True)
        largest = jnp.maximum(largest, 1e-30)
        scale = jnp.broadcast_to(32767.0 / largest, (8, LANES))
        slots = range(CENTER - left, CENTER + left + 1)
        for slot in slots:
            whole = []
            for h in range(2):
                scaled = surface_ref[slot, 8 * h : 8 * h + 8] * scale
                whole.append((scaled + jnp.where(scaled < 0, -0.5, 0.5)).astype(I32))
            table_ref[slot, 0:8] = pair_of(*whole)
        for slot in slots:
            value = pick(table_ref.at[slot], 8, lists_ref[slot].astype(I32))
            pairs = pair_of(value, pltpu.roll(value, 7, 0))
            table_ref[slot - 1, 9:10] = pairs[0:1]
            table_ref[slot + 1, 8:9] = pairs[2:3]
        return jnp.broadcast_to(largest * (1.0 / 32767.0), (8, LANES))

    def advance(left, unit):
        largest = jnp.zeros((8, LANES), F32)
        for slots in groups(left):
            for slot in slots:
                own_part = part(slot)
                for h in range(2):
                    rows = slice(8 * h, 8 * h + 8)
                    flow = None
                    for m in range(6):
                        first = 16 * m + 8 * h
                        near = pick(table_ref.at[slot], 10, own_part[first : first + 8].astype(I32)).astype(F32)
                        near = own_part[CONDUCT + first : CONDUCT + first + 8] * near
                        flow = near if flow is None else flow + near
                    keep = own_part[KEEP + 8 * h : KEEP + 8 * h + 8]
                    total = keep * surface_ref[slot, rows] + forcing_ref[slot - 2, rows] + flow * unit
                    surface_ref[slot, rows] = total
                    largest = jnp.maximum(largest, jnp.abs(total))
        return largest

    largest = jnp.zeros((8, LANES), F32)
    for slot in range(1, WINDOW + 3):
        for h in range(2):
            largest = jnp.maximum(largest, jnp.abs(surface_ref[slot, 8 * h : 8 * h + 8]))
    unit = spread(REACH + 1, largest)
    for left in reversed(range(STEPS)):
        largest = advance(left, unit)
        if left:
            unit = spread(left, largest)


def first_kernel(owner_ref, arrived_ref, low_ref, middle_ref, high_ref, out_ref, lists_ref, forcing_ref, terms_ref, surface_ref, table_ref):
    parts = (low_ref, middle_ref, high_ref)
    owner = owner_ref[0]
    for slot in range(1, WINDOW + 3):
        other = (owner + (slot - CENTER + OWNERS)) % OWNERS
        surface_ref[slot] = arrived_ref[other, 0:16]
        lists_ref[slot] = arrived_ref[other, 16:24]
    for slot in range(1, WINDOW + 3):
        lists_ref[slot, 4:8] = jnp.zeros((4, LANES), F32)
    blocks = lax.broadcasted_iota(I32, (16, TILES), 0)
    for k in range(WINDOW):
        for j in range(2):
            terms_ref[pl.ds(j, OWNERS, stride=2), :] = arrived_ref[:, TERMS + 2 * k + j, :]
        target = parts[k % 3][k // 3, TARGET : TARGET + 1, 0:TILES].astype(I32)
        hot = (blocks == target).astype(F32)
        forcing_ref[k] = jnp.dot(hot, terms_ref[...], precision=HIGHEST, preferred_element_type=F32)
    run_steps(parts, lists_ref, forcing_ref, surface_ref, table_ref)
    out_ref[...] = jnp.broadcast_to(surface_ref[CENTER][None], out_ref.shape)


def last_kernel(owner_ref, target_ref, surfaces_ref, low_ref, middle_ref, high_ref, lists_ref, forcing_ref, out_ref, values_ref, surface_ref, table_ref):
    parts = (low_ref, middle_ref, high_ref)
    owner = owner_ref[0]
    for slot in range(1, WINDOW + 3):
        surface_ref[slot] = surfaces_ref[(owner + (slot - CENTER + OWNERS)) % OWNERS]
    run_steps(parts, lists_ref, forcing_ref, surface_ref, table_ref)
    out_ref[...] = surface_ref[CENTER]
    for t in range(TILES):
        values_ref[t // 2, t % 2 : t % 2 + 1] = surface_ref[CENTER, pl.ds(target_ref[t], 1), :]


def shape(*dims):
    return jax.ShapeDtypeStruct(dims, F32)


def local(
    atm_flux,
    level_weight,
    tile_weight,
    tile_source,
    tile_target,
    ocean_start,
    conductance,
    damping,
    neighbors,
    send_lists,
):
    owner = lax.axis_index("cells").astype(I32).reshape(1)
    scratch = [
        pltpu.VMEM((SLOTS, 16, LANES), F32),
        pltpu.VMEM((SLOTS, 16, LANES), I32),
    ]

    partials, packed = pl.pallas_call(
        prepare_kernel,
        out_shape=(shape(8, 16, LANES), shape(PART, LANES)),
        in_specs=[SMEM] + [VMEM] * 7,
        scratch_shapes=[pltpu.VMEM((16, LANES), F32)],
    )(
        level_weight,
        atm_flux,
        neighbors,
        conductance,
        damping.reshape(16, LANES),
        ocean_start.reshape(16, LANES),
        send_lists,
        tile_target.reshape(1, TILES),
    )
    shares = lax.all_to_all(partials, "comp", split_axis=0, concat_axis=0, tiled=True)
    lower, higher = from_owner(packed, -3), from_owner(packed, 3)
    three = jnp.concatenate([lower, packed, higher], axis=0)
    terms = pl.pallas_call(
        terms_kernel,
        out_shape=shape(OWNERS, SENT, LANES),
        in_specs=[SMEM] + [VMEM] * 3,
        scratch_shapes=[pltpu.VMEM((16, 8, LANES), F32), pltpu.VMEM((TILES + 2 * WINDOW, LANES), F32)],
    )(tile_source, shares, packed, tile_weight)
    arrived = exchange(terms)
    lower, higher = from_owner(three, -1), from_owner(three, 1)
    window = [block.reshape(3, PART, LANES) for block in (lower, three, higher)]
    surface, lists, forcing = pl.pallas_call(
        first_kernel,
        out_shape=(shape(OWNERS, 16, LANES), shape(SLOTS, 8, LANES), shape(WINDOW, 16, LANES)),
        in_specs=[SMEM] + [VMEM] * 4,
        scratch_shapes=[pltpu.VMEM((TILES, LANES), F32)] + scratch,
    )(owner, arrived, *window)
    surfaces = exchange(surface)
    ocean_end, values = pl.pallas_call(
        last_kernel,
        out_shape=(shape(16, LANES), shape(OWNERS, 2, LANES)),
        in_specs=[SMEM] * 2 + [VMEM] * 6,
        scratch_shapes=scratch,
    )(owner, tile_target, surfaces, *window, lists, forcing)
    ocean_end = to_idle(ocean_end)
    returned = exchange(values).reshape(TILES, LANES)
    pulled = jnp.sum(returned[:, None, :] * tile_weight.astype(F32), axis=2)
    source_hot = (tile_source[:, None] == jnp.arange(16, dtype=I32)[None, :]).astype(F32)
    atm_back = jnp.einsum("ra,rb->ab", source_hot, pulled, precision=HIGHEST).reshape(-1)
    return (ocean_end.reshape(-1), to_idle(atm_back))


def solution(mesh):
    in_specs = (
        P("comp", "cells"),
        P("comp"),
        P("cells", None, None),
        P("cells"),
        P("cells"),
        P("cells"),
        P(None, "cells"),
        P("cells"),
        P(None, "cells"),
        P(None, "cells"),
    )
    out_specs = (P("cells"), P("cells"))
    return jax.shard_map(local, mesh=mesh, in_specs=in_specs, out_specs=out_specs, check_vma=False)
```

```python
import jax
import jax.numpy as jnp
from jax import lax
from jax.experimental import pallas as pl
from jax.experimental.pallas import tpu as pltpu
from jax.sharding import PartitionSpec as P


LANES = 128
OWNERS = 32
HALF = 16
TILES = 64
REACH = 4
STEPS = 5
WINDOW = 2 * REACH + 1
CENTER = REACH + 2
SLOTS = WINDOW + 4
PART = 232
CONDUCT, KEEP, START, LISTS, TARGET = 96, 192, 208, 224, 228
SENT = 40
TERMS = 22
BOTH = ("comp", "cells")
HIGHEST = lax.Precision.HIGHEST
F32, I32 = jnp.float32, jnp.int32
VMEM = pl.BlockSpec(memory_space=pltpu.VMEM)
SMEM = pl.BlockSpec(memory_space=pltpu.SMEM)


def device_of(owner, copy, core):
    z_low = copy if owner < HALF else 3 - copy
    return (2 * z_low + core) * OWNERS + owner


COPIES = [(0, 0), (3, 0)]
PLANES = [[(1, 0), (1, 1)], [(2, 0), (2, 1)], [(0, 1), (3, 1)]]
IDLE = [
    [(2 * z_low + core) * OWNERS + half * HALF + i for z_low, core in planes for i in range(HALF)]
    for planes in PLANES
    for half in range(2)
]
ALL = [[device_of(owner, *copy) for owner in range(OWNERS)] for copy in COPIES] + IDLE


def from_owner(block, offset):
    route = [
        (device_of((owner + offset) % OWNERS, *copy), device_of(owner, *copy))
        for copy in COPIES
        for owner in range(OWNERS)
    ]
    return lax.ppermute(block, BOTH, route)


def to_idle(block):
    arrived = []
    for aside, core in ((1, 0), (1, 1), (0, 1)):
        route = [
            (2 * here * OWNERS + owner, (2 * (there if aside else here) + core) * OWNERS + owner)
            for here, there in ((0, 1), (3, 2))
            for owner in range(OWNERS)
        ]
        arrived.append(lax.ppermute(block, BOTH, route))
    seat = lax.axis_index("comp")
    return jnp.where((seat == 0) | (seat == 6), block, arrived[0] + arrived[1] + arrived[2])


def exchange(blocks):
    return lax.all_to_all(blocks, BOTH, split_axis=0, concat_axis=0, tiled=True, axis_index_groups=ALL)


def lane_pick(rows, lane):
    dims = lax.GatherDimensionNumbers(
        offset_dims=(),
        collapsed_slice_dims=(1,),
        start_index_map=(1,),
        operand_batching_dims=(0,),
        start_indices_batching_dims=(0,),
    )
    return lax.gather(
        rows,
        lane[..., None],
        dims,
        slice_sizes=(1, 1),
        mode=lax.GatherScatterMode.PROMISE_IN_BOUNDS,
    )


def coded(index):
    row, lane = index >> 7, index & 127
    halo = row >= 16
    pair = jnp.where(halo, 8 + ((row >> 1) & 1), row & 7)
    half = jnp.where(halo, row & 1, row >> 3)
    return pair * 256 + half * 128 + lane


def pair_of(upper, lower):
    return (upper << 16) | (lower & 0xFFFF)


def pick(table_ref, count, code):
    lane, pair = code & 127, code >> 8
    total = None
    for r in range(count):
        line = table_ref[pl.ds(r, 8, stride=0), :]
        near = lane_pick(line, lane)
        total = near if total is None else jnp.where(pair == r, near, total)
    return jnp.where((code & 128) == 0, total, total << 16) >> 16


def prepare_kernel(weight_ref, flux_ref, neighbor_ref, conduct_ref, damping_ref, start_ref, lists_ref, target_ref, shares_ref, packed_ref, row_ref):
    for j in range(16):
        lanes = slice(LANES * j, LANES * j + LANES)
        block = flux_ref[:, lanes].astype(F32)
        row_ref[j : j + 1] = sum(weight_ref[level] * block[level : level + 1] for level in range(block.shape[0]))
    shares_ref[...] = jnp.broadcast_to(row_ref[...][None], shares_ref.shape)
    own = packed_ref
    for j in range(16):
        lanes = slice(LANES * j, LANES * j + LANES)
        own[pl.ds(j, 6, stride=16), :] = coded(neighbor_ref[:, lanes]).astype(F32)
        conduct = conduct_ref[:, lanes]
        own[pl.ds(CONDUCT + j, 6, stride=16), :] = conduct
        own[KEEP + j : KEEP + j + 1] = 1.0 - jnp.sum(conduct, axis=0, keepdims=True) - damping_ref[j : j + 1]
    own[START:LISTS] = start_ref[...]
    for j in range(2):
        lanes = slice(LANES * j, LANES * j + LANES)
        lists = coded(lists_ref[:, lanes]).astype(F32)
        own[LISTS + j : LISTS + j + 1] = lists[0:1]
        own[LISTS + 2 + j : LISTS + 3 + j] = lists[1:2]
    own[TARGET:PART] = jnp.zeros((PART - TARGET, LANES), F32)
    own[TARGET : TARGET + 1, 0:TILES] = target_ref[...].astype(F32)


def terms_kernel(source_ref, shares_ref, packed_ref, weight_ref, out_ref, parts_ref, terms_ref):
    flux = jnp.sum(shares_ref[...], axis=0)
    high = flux.astype(jnp.bfloat16).astype(F32)
    rest = flux - high
    middle = rest.astype(jnp.bfloat16).astype(F32)
    parts_ref[...] = jnp.zeros_like(parts_ref)
    parts_ref[:, 0, :] = high
    parts_ref[:, 1, :] = middle
    parts_ref[:, 2, :] = rest - middle
    for t in range(TILES):
        left = parts_ref[source_ref[t]].astype(jnp.bfloat16)
        three = jnp.dot(left, weight_ref[t], preferred_element_type=F32)
        term = jnp.sum(three, axis=0, keepdims=True)
        place = (t + 2 * REACH) % TILES
        while place < TILES + 2 * WINDOW:
            terms_ref[place : place + 1] = term
            place += TILES
    fixed = packed_ref[START : START + 24]
    for p in range(OWNERS):
        out_ref[p, 0:24] = fixed
        out_ref[p, TERMS:SENT] = terms_ref[2 * p : 2 * p + 2 * WINDOW]


def groups(left):
    if left == 0:
        return [[CENTER]]
    pairs = [[CENTER - i, CENTER + i] for i in range(2, left + 1)]
    return [[CENTER, CENTER - 1, CENTER + 1]] + pairs


def run_steps(parts, lists_ref, forcing_ref, surface_ref, table_ref):
    def part(slot):
        return parts[(slot - 2) // 3].at[(slot - 2) % 3]

    def spread(left, largest):
        largest = jnp.max(jnp.max(largest, axis=1, keepdims=True), axis=0, keepdims=True)
        largest = jnp.maximum(largest, 1e-30)
        scale = jnp.broadcast_to(32767.0 / largest, (8, LANES))
        slots = range(CENTER - left, CENTER + left + 1)
        for slot in slots:
            whole = []
            for h in range(2):
                scaled = surface_ref[slot, 8 * h : 8 * h + 8] * scale
                whole.append((scaled + jnp.where(scaled < 0, -0.5, 0.5)).astype(I32))
            table_ref[slot, 0:8] = pair_of(*whole)
        for slot in slots:
            value = pick(table_ref.at[slot], 8, lists_ref[slot].astype(I32))
            pairs = pair_of(value, pltpu.roll(value, 7, 0))
            table_ref[slot - 1, 9:10] = pairs[0:1]
            table_ref[slot + 1, 8:9] = pairs[2:3]
        return jnp.broadcast_to(largest * (1.0 / 32767.0), (8, LANES))

    def advance(left, unit):
        largest = jnp.zeros((8, LANES), F32)
        for slots in groups(left):
            for slot in slots:
                own_part = part(slot)
                for h in range(2):
                    rows = slice(8 * h, 8 * h + 8)
                    flow = None
                    for m in range(6):
                        first = 16 * m + 8 * h
                        near = pick(table_ref.at[slot], 10, own_part[first : first + 8].astype(I32)).astype(F32)
                        near = own_part[CONDUCT + first : CONDUCT + first + 8] * near
                        flow = near if flow is None else flow + near
                    keep = own_part[KEEP + 8 * h : KEEP + 8 * h + 8]
                    total = keep * surface_ref[slot, rows] + forcing_ref[slot - 2, rows] + flow * unit
                    surface_ref[slot, rows] = total
                    largest = jnp.maximum(largest, jnp.abs(total))
        return largest

    largest = jnp.zeros((8, LANES), F32)
    for slot in range(1, WINDOW + 3):
        for h in range(2):
            largest = jnp.maximum(largest, jnp.abs(surface_ref[slot, 8 * h : 8 * h + 8]))
    unit = spread(REACH + 1, largest)
    for left in reversed(range(STEPS)):
        largest = advance(left, unit)
        if left:
            unit = spread(left, largest)


def first_kernel(owner_ref, arrived_ref, low_ref, middle_ref, high_ref, out_ref, lists_ref, forcing_ref, terms_ref, surface_ref, table_ref):
    parts = (low_ref, middle_ref, high_ref)
    owner = owner_ref[0]
    for slot in range(1, WINDOW + 3):
        other = (owner + (slot - CENTER + OWNERS)) % OWNERS
        surface_ref[slot] = arrived_ref[other, 0:16]
        lists_ref[slot] = arrived_ref[other, 16:24]
    for slot in range(1, WINDOW + 3):
        lists_ref[slot, 4:8] = jnp.zeros((4, LANES), F32)
    blocks = lax.broadcasted_iota(I32, (16, TILES), 0)
    for k in range(WINDOW):
        for j in range(2):
            terms_ref[pl.ds(j, OWNERS, stride=2), :] = arrived_ref[:, TERMS + 2 * k + j, :]
        target = parts[k // 3][k % 3, TARGET : TARGET + 1, 0:TILES].astype(I32)
        hot = (blocks == target).astype(F32)
        forcing_ref[k] = jnp.dot(hot, terms_ref[...], precision=HIGHEST, preferred_element_type=F32)
    run_steps(parts, lists_ref, forcing_ref, surface_ref, table_ref)
    out_ref[...] = jnp.broadcast_to(surface_ref[CENTER][None], out_ref.shape)


def last_kernel(owner_ref, target_ref, surfaces_ref, low_ref, middle_ref, high_ref, lists_ref, forcing_ref, out_ref, values_ref, surface_ref, table_ref):
    parts = (low_ref, middle_ref, high_ref)
    owner = owner_ref[0]
    for slot in range(1, WINDOW + 3):
        surface_ref[slot] = surfaces_ref[(owner + (slot - CENTER + OWNERS)) % OWNERS]
    run_steps(parts, lists_ref, forcing_ref, surface_ref, table_ref)
    out_ref[...] = surface_ref[CENTER]
    for t in range(TILES):
        values_ref[t // 2, t % 2 : t % 2 + 1] = surface_ref[CENTER, pl.ds(target_ref[t], 1), :]


def shape(*dims):
    return jax.ShapeDtypeStruct(dims, F32)


def local(
    atm_flux,
    level_weight,
    tile_weight,
    tile_source,
    tile_target,
    ocean_start,
    conductance,
    damping,
    neighbors,
    send_lists,
):
    owner = lax.axis_index("cells").astype(I32).reshape(1)
    scratch = [
        pltpu.VMEM((SLOTS, 16, LANES), F32),
        pltpu.VMEM((SLOTS, 16, LANES), I32),
    ]

    partials, packed = pl.pallas_call(
        prepare_kernel,
        out_shape=(shape(8, 16, LANES), shape(PART, LANES)),
        in_specs=[SMEM] + [VMEM] * 7,
        scratch_shapes=[pltpu.VMEM((16, LANES), F32)],
    )(
        level_weight,
        atm_flux,
        neighbors,
        conductance,
        damping.reshape(16, LANES),
        ocean_start.reshape(16, LANES),
        send_lists,
        tile_target.reshape(1, TILES),
    )
    shares = lax.all_to_all(partials, "comp", split_axis=0, concat_axis=0, tiled=True)
    lower, higher = from_owner(packed, -1), from_owner(packed, 1)
    three = jnp.concatenate([lower, packed, higher], axis=0)
    terms = pl.pallas_call(
        terms_kernel,
        out_shape=shape(OWNERS, SENT, LANES),
        in_specs=[SMEM] + [VMEM] * 3,
        scratch_shapes=[pltpu.VMEM((16, 8, LANES), F32), pltpu.VMEM((TILES + 2 * WINDOW, LANES), F32)],
    )(tile_source, shares, packed, tile_weight)
    arrived = exchange(terms)
    lower, higher = from_owner(three, -3), from_owner(three, 3)
    window = [block.reshape(3, PART, LANES) for block in (lower, three, higher)]
    surface, lists, forcing = pl.pallas_call(
        first_kernel,
        out_shape=(shape(OWNERS, 16, LANES), shape(SLOTS, 8, LANES), shape(WINDOW, 16, LANES)),
        in_specs=[SMEM] + [VMEM] * 4,
        scratch_shapes=[pltpu.VMEM((TILES, LANES), F32)] + scratch,
    )(owner, arrived, *window)
    surfaces = exchange(surface)
    ocean_end, values = pl.pallas_call(
        last_kernel,
        out_shape=(shape(16, LANES), shape(OWNERS, 2, LANES)),
        in_specs=[SMEM] * 2 + [VMEM] * 6,
        scratch_shapes=scratch,
    )(owner, tile_target, surfaces, *window, lists, forcing)
    ocean_end = to_idle(ocean_end)
    returned = exchange(values).reshape(TILES, LANES)
    pulled = jnp.sum(returned[:, None, :] * tile_weight.astype(F32), axis=2)
    source_hot = (tile_source[:, None] == jnp.arange(16, dtype=I32)[None, :]).astype(F32)
    atm_back = jnp.einsum("ra,rb->ab", source_hot, pulled, precision=HIGHEST).reshape(-1)
    return (ocean_end.reshape(-1), to_idle(atm_back))


def solution(mesh):
    in_specs = (
        P("comp", "cells"),
        P("comp"),
        P("cells", None, None),
        P("cells"),
        P("cells"),
        P("cells"),
        P(None, "cells"),
        P("cells"),
        P(None, "cells"),
        P(None, "cells"),
    )
    out_specs = (P("cells"), P("cells"))
    return jax.shard_map(local, mesh=mesh, in_specs=in_specs, out_specs=out_specs, check_vma=False)
```

```python
import jax
import jax.numpy as jnp
from jax import lax
from jax.experimental import pallas as pl
from jax.experimental.pallas import tpu as pltpu
from jax.sharding import PartitionSpec as P


LANES = 128
OWNERS = 32
HALF = 16
TILES = 64
REACH = 4
STEPS = 5
WINDOW = 2 * REACH + 1
CENTER = REACH + 2
SLOTS = WINDOW + 4
PART = 216
CONDUCT, KEEP, TARGET = 96, 192, 208
SENT = 40
TERMS = 22
BOTH = ("comp", "cells")
HIGHEST = lax.Precision.HIGHEST
F32, I32 = jnp.float32, jnp.int32
VMEM = pl.BlockSpec(memory_space=pltpu.VMEM)
SMEM = pl.BlockSpec(memory_space=pltpu.SMEM)


def device_of(owner, copy, core):
    z_low = copy if owner < HALF else 3 - copy
    return (2 * z_low + core) * OWNERS + owner


COPIES = [(copy, core) for copy in (0, 3) for core in range(2)]
IDLE = [
    [(2 * z_low + core) * OWNERS + half * HALF + i for core in range(2) for i in range(HALF)]
    for z_low in (1, 2)
    for half in range(2)
]
ALL = [[device_of(owner, *copy) for owner in range(OWNERS)] for copy in COPIES] + IDLE


def from_owner(block, offset):
    route = [
        (device_of((owner + offset) % OWNERS, *copy), device_of(owner, *copy))
        for copy in COPIES
        for owner in range(OWNERS)
    ]
    return lax.ppermute(block, BOTH, route)


def to_idle(block):
    route = [
        ((2 * here + core) * OWNERS + owner, (2 * there + core) * OWNERS + owner)
        for here, there in ((0, 1), (3, 2))
        for core in range(2)
        for owner in range(OWNERS)
    ]
    z_low = lax.axis_index("comp") // 2
    return jnp.where((z_low == 0) | (z_low == 3), block, lax.ppermute(block, BOTH, route))


def exchange(blocks):
    return lax.all_to_all(blocks, BOTH, split_axis=0, concat_axis=0, tiled=True, axis_index_groups=ALL)


def lane_pick(rows, lane):
    dims = lax.GatherDimensionNumbers(
        offset_dims=(),
        collapsed_slice_dims=(1,),
        start_index_map=(1,),
        operand_batching_dims=(0,),
        start_indices_batching_dims=(0,),
    )
    return lax.gather(
        rows,
        lane[..., None],
        dims,
        slice_sizes=(1, 1),
        mode=lax.GatherScatterMode.PROMISE_IN_BOUNDS,
    )


def coded(index):
    row, lane = index >> 7, index & 127
    halo = row >= 16
    pair = jnp.where(halo, 8 + ((row >> 1) & 1), row & 7)
    half = jnp.where(halo, row & 1, row >> 3)
    return pair * 256 + half * 128 + lane


def pair_of(upper, lower):
    return (upper << 16) | (lower & 0xFFFF)


def pick(table_ref, count, code):
    lane, pair = code & 127, code >> 8
    total = None
    for r in range(count):
        line = table_ref[pl.ds(r, 8, stride=0), :]
        near = lane_pick(line, lane)
        total = near if total is None else jnp.where(pair == r, near, total)
    return jnp.where((code & 128) == 0, total, total << 16) >> 16


def prepare_kernel(weight_ref, flux_ref, neighbor_ref, conduct_ref, damping_ref, start_ref, lists_ref, target_ref, shares_ref, packed_ref, fixed_ref, row_ref):
    for j in range(16):
        lanes = slice(LANES * j, LANES * j + LANES)
        block = flux_ref[:, lanes].astype(F32)
        row_ref[j : j + 1] = sum(weight_ref[level] * block[level : level + 1] for level in range(block.shape[0]))
    shares_ref[...] = jnp.broadcast_to(row_ref[...][None], shares_ref.shape)
    own = packed_ref
    for j in range(16):
        lanes = slice(LANES * j, LANES * j + LANES)
        own[pl.ds(j, 6, stride=16), :] = coded(neighbor_ref[:, lanes]).astype(F32)
        conduct = conduct_ref[:, lanes]
        own[pl.ds(CONDUCT + j, 6, stride=16), :] = conduct
        own[KEEP + j : KEEP + j + 1] = 1.0 - jnp.sum(conduct, axis=0, keepdims=True) - damping_ref[j : j + 1]
    fixed_ref[0:16] = start_ref[...]
    for j in range(2):
        lanes = slice(LANES * j, LANES * j + LANES)
        lists = coded(lists_ref[:, lanes]).astype(F32)
        fixed_ref[16 + j : 17 + j] = lists[0:1]
        fixed_ref[18 + j : 19 + j] = lists[1:2]
    fixed_ref[20:24] = jnp.zeros((4, LANES), F32)
    own[TARGET:PART] = jnp.zeros((PART - TARGET, LANES), F32)
    own[TARGET : TARGET + 1, 0:TILES] = target_ref[...].astype(F32)


def terms_kernel(source_ref, shares_ref, fixed_ref, weight_ref, out_ref, parts_ref, terms_ref):
    flux = jnp.sum(shares_ref[...], axis=0)
    high = flux.astype(jnp.bfloat16).astype(F32)
    rest = flux - high
    middle = rest.astype(jnp.bfloat16).astype(F32)
    parts_ref[...] = jnp.zeros_like(parts_ref)
    parts_ref[:, 0, :] = high
    parts_ref[:, 1, :] = middle
    parts_ref[:, 2, :] = rest - middle
    for t in range(TILES):
        left = parts_ref[source_ref[t]].astype(jnp.bfloat16)
        three = jnp.dot(left, weight_ref[t], preferred_element_type=F32)
        term = jnp.sum(three, axis=0, keepdims=True)
        place = (t + 2 * REACH) % TILES
        while place < TILES + 2 * WINDOW:
            terms_ref[place : place + 1] = term
            place += TILES
    fixed = fixed_ref[...]
    for p in range(OWNERS):
        out_ref[p, 0:24] = fixed
        out_ref[p, TERMS:SENT] = terms_ref[2 * p : 2 * p + 2 * WINDOW]


def groups(left):
    if left == 0:
        return [[CENTER]]
    pairs = [[CENTER - i, CENTER + i] for i in range(2, left + 1)]
    return [[CENTER, CENTER - 1, CENTER + 1]] + pairs


def run_steps(parts, lists_ref, forcing_ref, surface_ref, table_ref):
    def part(slot):
        return parts[(slot - 2) // 3].at[(slot - 2) % 3]

    def spread(left, largest):
        largest = jnp.max(jnp.max(largest, axis=1, keepdims=True), axis=0, keepdims=True)
        largest = jnp.maximum(largest, 1e-30)
        scale = jnp.broadcast_to(32767.0 / largest, (8, LANES))
        slots = range(CENTER - left, CENTER + left + 1)
        for slot in slots:
            whole = []
            for h in range(2):
                scaled = surface_ref[slot, 8 * h : 8 * h + 8] * scale
                whole.append((scaled + jnp.where(scaled < 0, -0.5, 0.5)).astype(I32))
            table_ref[slot, 0:8] = pair_of(*whole)
        for slot in slots:
            value = pick(table_ref.at[slot], 8, lists_ref[slot].astype(I32))
            pairs = pair_of(value, pltpu.roll(value, 7, 0))
            table_ref[slot - 1, 9:10] = pairs[0:1]
            table_ref[slot + 1, 8:9] = pairs[2:3]
        return jnp.broadcast_to(largest * (1.0 / 32767.0), (8, LANES))

    def advance(left, unit):
        largest = jnp.zeros((8, LANES), F32)
        for slots in groups(left):
            for slot in slots:
                own_part = part(slot)
                for h in range(2):
                    rows = slice(8 * h, 8 * h + 8)
                    flow = None
                    for m in range(6):
                        first = 16 * m + 8 * h
                        near = pick(table_ref.at[slot], 10, own_part[first : first + 8].astype(I32)).astype(F32)
                        near = own_part[CONDUCT + first : CONDUCT + first + 8] * near
                        flow = near if flow is None else flow + near
                    keep = own_part[KEEP + 8 * h : KEEP + 8 * h + 8]
                    total = keep * surface_ref[slot, rows] + forcing_ref[slot - 2, rows] + flow * unit
                    surface_ref[slot, rows] = total
                    largest = jnp.maximum(largest, jnp.abs(total))
        return largest

    largest = jnp.zeros((8, LANES), F32)
    for slot in range(1, WINDOW + 3):
        for h in range(2):
            largest = jnp.maximum(largest, jnp.abs(surface_ref[slot, 8 * h : 8 * h + 8]))
    unit = spread(REACH + 1, largest)
    for left in reversed(range(STEPS)):
        largest = advance(left, unit)
        if left:
            unit = spread(left, largest)


def first_kernel(owner_ref, arrived_ref, low_ref, middle_ref, high_ref, out_ref, lists_ref, forcing_ref, terms_ref, surface_ref, table_ref):
    parts = (low_ref, middle_ref, high_ref)
    owner = owner_ref[0]
    for slot in range(1, WINDOW + 3):
        other = (owner + (slot - CENTER + OWNERS)) % OWNERS
        surface_ref[slot] = arrived_ref[other, 0:16]
        lists_ref[slot] = arrived_ref[other, 16:24]
    for slot in range(1, WINDOW + 3):
        lists_ref[slot, 4:8] = jnp.zeros((4, LANES), F32)
    blocks = lax.broadcasted_iota(I32, (16, TILES), 0)
    for k in range(WINDOW):
        for j in range(2):
            terms_ref[pl.ds(j, OWNERS, stride=2), :] = arrived_ref[:, TERMS + 2 * k + j, :]
        target = parts[k // 3][k % 3, TARGET : TARGET + 1, 0:TILES].astype(I32)
        hot = (blocks == target).astype(F32)
        forcing_ref[k] = jnp.dot(hot, terms_ref[...], precision=HIGHEST, preferred_element_type=F32)
    run_steps(parts, lists_ref, forcing_ref, surface_ref, table_ref)
    out_ref[...] = jnp.broadcast_to(surface_ref[CENTER][None], out_ref.shape)


def last_kernel(owner_ref, target_ref, surfaces_ref, low_ref, middle_ref, high_ref, lists_ref, forcing_ref, out_ref, values_ref, surface_ref, table_ref):
    parts = (low_ref, middle_ref, high_ref)
    owner = owner_ref[0]
    for slot in range(1, WINDOW + 3):
        surface_ref[slot] = surfaces_ref[(owner + (slot - CENTER + OWNERS)) % OWNERS]
    run_steps(parts, lists_ref, forcing_ref, surface_ref, table_ref)
    out_ref[...] = surface_ref[CENTER]
    for t in range(TILES):
        values_ref[t // 2, t % 2 : t % 2 + 1] = surface_ref[CENTER, pl.ds(target_ref[t], 1), :]


def shape(*dims):
    return jax.ShapeDtypeStruct(dims, F32)


def local(
    atm_flux,
    level_weight,
    tile_weight,
    tile_source,
    tile_target,
    ocean_start,
    conductance,
    damping,
    neighbors,
    send_lists,
):
    owner = lax.axis_index("cells").astype(I32).reshape(1)
    scratch = [
        pltpu.VMEM((SLOTS, 16, LANES), F32),
        pltpu.VMEM((SLOTS, 16, LANES), I32),
    ]

    partials, packed, fixed = pl.pallas_call(
        prepare_kernel,
        out_shape=(shape(8, 16, LANES), shape(PART, LANES), shape(24, LANES)),
        in_specs=[SMEM] + [VMEM] * 7,
        scratch_shapes=[pltpu.VMEM((16, LANES), F32)],
    )(
        level_weight,
        atm_flux,
        neighbors,
        conductance,
        damping.reshape(16, LANES),
        ocean_start.reshape(16, LANES),
        send_lists,
        tile_target.reshape(1, TILES),
    )
    shares = lax.all_to_all(partials, "comp", split_axis=0, concat_axis=0, tiled=True)
    lower, higher = from_owner(packed, -1), from_owner(packed, 1)
    three = jnp.concatenate([lower, packed, higher], axis=0)
    terms = pl.pallas_call(
        terms_kernel,
        out_shape=shape(OWNERS, SENT, LANES),
        in_specs=[SMEM] + [VMEM] * 3,
        scratch_shapes=[pltpu.VMEM((16, 8, LANES), F32), pltpu.VMEM((TILES + 2 * WINDOW, LANES), F32)],
    )(tile_source, shares, fixed, tile_weight)
    arrived = exchange(terms)
    lower, higher = from_owner(three, -3), from_owner(three, 3)
    window = [block.reshape(3, PART, LANES) for block in (lower, three, higher)]
    surface, lists, forcing = pl.pallas_call(
        first_kernel,
        out_shape=(shape(OWNERS, 16, LANES), shape(SLOTS, 8, LANES), shape(WINDOW, 16, LANES)),
        in_specs=[SMEM] + [VMEM] * 4,
        scratch_shapes=[pltpu.VMEM((TILES, LANES), F32)] + scratch,
    )(owner, arrived, *window)
    surfaces = exchange(surface)
    ocean_end, values = pl.pallas_call(
        last_kernel,
        out_shape=(shape(16, LANES), shape(OWNERS, 2, LANES)),
        in_specs=[SMEM] * 2 + [VMEM] * 6,
        scratch_shapes=scratch,
    )(owner, tile_target, surfaces, *window, lists, forcing)
    returned = exchange(values)
    ocean_end = to_idle(ocean_end)
    returned, ocean_end = lax.optimization_barrier((returned, ocean_end))
    returned = returned.reshape(TILES, LANES)
    pulled = jnp.sum(returned[:, None, :] * tile_weight.astype(F32), axis=2)
    source_hot = (tile_source[:, None] == jnp.arange(16, dtype=I32)[None, :]).astype(F32)
    atm_back = jnp.einsum("ra,rb->ab", source_hot, pulled, precision=HIGHEST).reshape(-1)
    return (ocean_end.reshape(-1), to_idle(atm_back))


def solution(mesh):
    in_specs = (
        P("comp", "cells"),
        P("comp"),
        P("cells", None, None),
        P("cells"),
        P("cells"),
        P("cells"),
        P(None, "cells"),
        P("cells"),
        P(None, "cells"),
        P(None, "cells"),
    )
    out_specs = (P("cells"), P("cells"))
    return jax.shard_map(local, mesh=mesh, in_specs=in_specs, out_specs=out_specs, check_vma=False)
```
